256 devices in a mesh: tgt: 32 (over z, y_hi, core), src: 8 (over y_lo, x).
Axes of the slice: x: 4, y: 4 (y_hi: 2, y_lo: 2; y = y_hi * 2 + y_lo), z: 8, core: 2. Of those that a mesh axis runs over, the one named last changes fastest.
Arguments:
- tgt_points: bfloat16 [3, 16384], P(None, 'tgt'), may hold values from -4 to 4
- tgt_weight: float32 [16384], P('tgt'), may hold values from 0.5 to 2
- src_points: bfloat16 [4, 3, 32768], P(None, None, ('tgt', 'src')), may hold values from -4 to 4
- src_weight: float32 [4, 32768], P(None, ('tgt', 'src')), may hold values from 0.5 to 2
- basis: float32 [4, 3, 32768], P(None, None, ('tgt', 'src')), may hold values from 0.05 to 1
- span: int32 [4, 32768], P(None, ('tgt', 'src')), may hold values from 0 to 29
- patch: int32 [4, 32768], P(None, ('tgt', 'src')), may hold values from 0 to 3
- patch_factor: float32 [4, 2, 1024], P(None, None, ('tgt', 'src')), may hold values from -1.5 to 1.5
- ctrl_weight: float32 [4, 8192], P(None, ('tgt', 'src')), may hold values from 0.5 to 2
- ctrl_coef: bfloat16 [4, 128, 8192], P(None, None, ('tgt', 'src')), may hold values from -6 to 6
- band: float32 [8, 16384], P(None, 'tgt'), may hold values from -0.5 to 0.5
- offsets: int32 [8], replicated, may hold values from -8 to 8, as said below
Outputs:
- shell_field: float32 [16384, 128], P('tgt')
The draws below stay inside these ranges and needn't reach their ends.
Inputs may be any that keep to these rules, and one draw needn't show every extreme that they name: span of source point j is local to the 32 control points of the block j // 128. patch of source point j is local to the 4 patches of the block j // 128. offsets[0] is 8 and offsets[1] is -8.
All inputs are finite; a program needn't handle non-finite values.
Results may differ from the reference program's by a relative error of at most 0.0041.
Values may be sent and summed in bfloat16 or wider, within the bound.
No kernel may reach another device: no remote copies, remote signals or barrier semaphores. Data moves between devices by JAX's collectives and lax.ppermute only.
A program may use at most 128 MiB of HBM per device.

```python
import math
import jax
import jax.numpy as jnp
from jax import lax

SRC_DEV = 128
ROUNDS = 4
NRHS = 64
DEGREE = 2
PATCH_DEV = 4
HALO = 8
NB = 8
ORDER = 3
CTRL_DEV = 32
TARGETS = 16384
SOURCES = 32768
CONTROLS = 8192
PATCHES = 1024


def draw_offsets(key, part):
    values = jax.random.randint(key, (NB,), -HALO, HALO + 1)
    values = values.at[0].set(HALO).at[1].set(-HALO)
    return values.astype(jnp.int32)


def touch_ends(array, rng, least, high):
    shape = array.shape
    place = [jax.random.randint(jax.random.fold_in(rng, axis), (), 0, shape[axis]) for axis in range(len(shape))]
    array = array.at[tuple(place)].set(least)
    longest = shape.index(max(shape))
    place[longest] = (place[longest] + 1) % shape[longest]
    return array.at[tuple(place)].set(high)


def steps_of(key, extent, pieces, smallest, top_value):
    factor_of = 1.0
    for axis_at, shards_of in pieces:
        draws = jax.random.uniform(jax.random.fold_in(jax.random.fold_in(key, 6), axis_at), (shards_of,), jnp.float32, smallest / len(pieces), top_value / len(pieces))
        factor_of = factor_of * jnp.repeat(jnp.exp(draws), extent[axis_at] // shards_of).reshape((-1,) + (1,) * (len(extent) - 1 - axis_at))
    return factor_of


def scatter_about(own_key, extent, width, bound, split=(), held_as=jnp.bfloat16):
    gain = steps_of(own_key, extent, split, -0.22, 0.18) if split else 1.0
    result = jax.random.normal(own_key, extent, jnp.float32) * width * gain
    return jnp.minimum(jnp.maximum(result, -bound), bound).astype(held_as)


def setup_inputs(seed: int = 0) -> dict:
    arg_keys = jax.random.split(jax.random.key(seed), 13)
    tgt_points = scatter_about(arg_keys[0], (3, TARGETS), 1.0, 4.0, ((1, 32),))
    tgt_weight = jnp.clip(jnp.exp(math.log(2.0) - 1.3862944 * jax.random.uniform(arg_keys[1], (TARGETS,), jnp.float32) ** steps_of(arg_keys[1], (TARGETS,), ((0, 32),), -0.2, 0.2)), 0.5, 2.0)
    src_points = scatter_about(arg_keys[2], (ROUNDS, 3, SOURCES), 1.0, 4.0, ((2, 256),))
    src_weight = jnp.clip(jnp.exp(math.log(2.0) - 1.3862944 * jax.random.uniform(arg_keys[3], (ROUNDS, SOURCES), jnp.float32) ** steps_of(arg_keys[3], (ROUNDS, SOURCES), ((1, 256),), -0.2, 0.2)), 0.5, 2.0)
    basis = jnp.clip(0.05 + 0.95 * jax.random.uniform(arg_keys[4], (ROUNDS, ORDER, SOURCES), jnp.float32) ** steps_of(arg_keys[4], (ROUNDS, ORDER, SOURCES), ((2, 256),), -0.2, 0.2), 0.05, 1.0)
    span = touch_ends(jax.random.randint(arg_keys[5], (ROUNDS, SOURCES), 0, CTRL_DEV - DEGREE), jax.random.fold_in(arg_keys[5], 1), 0, (CTRL_DEV - DEGREE) - 1).astype(jnp.int32)
    patch = touch_ends(jax.random.randint(arg_keys[6], (ROUNDS, SOURCES), 0, PATCH_DEV), jax.random.fold_in(arg_keys[6], 1), 0, PATCH_DEV - 1).astype(jnp.int32)
    patch_factor = jnp.clip(jax.random.uniform(arg_keys[7], (ROUNDS, 2, PATCHES), jnp.float32, -1.5, 1.5) * steps_of(arg_keys[7], (ROUNDS, 2, PATCHES), ((2, 256),), -0.4, 0.0), -1.5, 1.5)
    ctrl_weight = jnp.clip(jnp.exp(math.log(2.0) - 1.3862944 * jax.random.uniform(arg_keys[8], (ROUNDS, CONTROLS), jnp.float32) ** steps_of(arg_keys[8], (ROUNDS, CONTROLS), ((1, 256),), -0.2, 0.2)), 0.5, 2.0)
    ctrl_coef = scatter_about(arg_keys[9], (ROUNDS, 2 * NRHS, CONTROLS), 1.0, 6.0, ((2, 256),))
    band = jnp.clip(jax.random.uniform(arg_keys[10], (NB, TARGETS), jnp.float32, -0.5, 0.5) * steps_of(arg_keys[10], (NB, TARGETS), ((1, 32),), -0.4, 0.0), -0.5, 0.5)
    offsets = draw_offsets(jax.random.fold_in(arg_keys[12], 71), 0)
    return {"tgt_points": tgt_points, "tgt_weight": tgt_weight, "src_points": src_points, "src_weight": src_weight, "basis": basis, "span": span, "patch": patch, "patch_factor": patch_factor, "ctrl_weight": ctrl_weight, "ctrl_coef": ctrl_coef, "band": band, "offsets": offsets}


WAVE = 8.0
SMOOTH = 0.0025

def kernel_terms(targets, sources, density):
    tpos = targets.astype(jnp.float32)
    spos = sources.astype(jnp.float32)
    dist_sq = SMOOTH + (tpos[0][:, None] - spos[0][None, :]) ** 2
    dist_sq = dist_sq + (tpos[1][:, None] - spos[1][None, :]) ** 2
    dist_sq = dist_sq + (tpos[2][:, None] - spos[2][None, :]) ** 2
    dist = jnp.sqrt(dist_sq)
    kernel_re = (jnp.cos(WAVE * dist) / dist).astype(jnp.bfloat16)
    kernel_im = (jnp.sin(WAVE * dist) / dist).astype(jnp.bfloat16)
    dims = (((1,), (1,)), ((), ()))
    part_a = lax.dot_general(kernel_re.astype(jnp.float32), density.astype(jnp.float32), dims)
    part_b = lax.dot_general(kernel_im.astype(jnp.float32), density.astype(jnp.float32), dims)
    half = density.shape[0] // 2
    return jnp.concatenate([part_a[:, :half] - part_b[:, half:], part_a[:, half:] + part_b[:, :half]], axis=1)

def round_density(section, src_weight, basis, span, patch, patch_factor, ctrl_weight, ctrl_coef):
    count = src_weight.shape[1]
    block = jnp.arange(count, dtype=jnp.int32) // SRC_DEV
    base = block * CTRL_DEV + span[section]
    denom = jnp.zeros((count,), jnp.float32)
    numer = jnp.zeros((ctrl_coef.shape[1], count), jnp.float32)
    for basis_index in range(ORDER):
        control_index = (base + basis_index).astype(jnp.int32)
        scaled = basis[section, basis_index] * ctrl_weight[section][control_index]
        denom = denom + scaled
        numer = numer + scaled[None, :] * ctrl_coef[section][:, control_index].astype(jnp.float32)
    ratio = numer / denom[None, :]
    factor_index = (block * PATCH_DEV + patch[section]).astype(jnp.int32)
    factor_re = patch_factor[section, 0][factor_index]
    factor_im = patch_factor[section, 1][factor_index]
    ratio_re = ratio[:NRHS]
    ratio_im = ratio[NRHS:]
    weight = src_weight[section]
    dens_re = weight * (factor_re * ratio_re - factor_im * ratio_im)
    dens_im = weight * (factor_re * ratio_im + factor_im * ratio_re)
    return jnp.concatenate([dens_re, dens_im], axis=0).astype(jnp.bfloat16)

def reference(tgt_points, tgt_weight, src_points, src_weight, basis, span, patch, patch_factor, ctrl_weight, ctrl_coef, band, offsets):
    count = src_weight.shape[1]
    block_size = math.gcd(count, 2048)
    total = jnp.zeros((TARGETS, 2 * NRHS), jnp.float32)
    for section in range(ROUNDS):
        density = round_density(section, src_weight, basis, span, patch, patch_factor, ctrl_weight, ctrl_coef)
        sources = src_points[section]

        def step_fn(index, carried):
            start = (index * block_size).astype(jnp.int32)
            piece_src = lax.dynamic_slice_in_dim(sources, start, block_size, 1)
            piece_den = lax.dynamic_slice_in_dim(density, start, block_size, 1)
            return carried + kernel_terms(tgt_points, piece_src, piece_den)
        total = lax.fori_loop(0, count // block_size, step_fn, total)
    scale = jnp.float32(1.0 / math.sqrt(ROUNDS * SOURCES))
    potential = total * scale * tgt_weight[:, None]
    padded = jnp.pad(potential, ((HALO, HALO), (0, 0)))
    shell_field = potential
    for diag in range(NB):
        start = (HALO + offsets[diag]).astype(jnp.int32)
        rows = lax.dynamic_slice_in_dim(padded, start, TARGETS, 0)
        shell_field = shell_field + band[diag][:, None] * rows
    return shell_field
```

```python
import functools
import math

import jax
import jax.numpy as jnp
import numpy as np
from jax import lax
from jax.experimental import pallas as pl
from jax.experimental.pallas import tpu as pltpu
from jax.sharding import Mesh, PartitionSpec as P

HALO = 8
WAVE = 8.0
SMOOTH = 0.0025
TURN = WAVE / (2.0 * math.pi)
TURN_SQ = TURN * TURN

TGT = ("z", "yh", "core")
SRC = ("yl", "x")

SIN_POLY = ()
COS_POLY = ()


def minimax(func, terms, odd):
    nodes = 0.25 + 0.25 * np.cos(np.linspace(0.0, np.pi, 2001))
    nodes = nodes[nodes > 1e-6]
    scale = nodes if odd else np.ones_like(nodes)
    basis = np.stack([nodes ** (2 * k) for k in range(terms)], 1)
    value = func(nodes) / scale
    weight = np.ones_like(nodes)
    for _ in range(60):
        rows = scale * weight
        coef = np.linalg.lstsq(basis * rows[:, None], value * rows, rcond=None)[0]
        error = np.abs((basis @ coef - value) * scale)
        weight = weight * np.sqrt(1e-12 + error / error.max())
        weight = weight / weight.mean()
    return tuple(float(np.float32(c)) for c in coef)


SIN_POLY = minimax(lambda f: math.sqrt(2.0) * np.sin(np.pi * f), 3, True)
COS_POLY = minimax(lambda f: math.sqrt(2.0) * np.cos(np.pi * f), 4, False)


def horner(z, coef):
    value = coef[-1]
    for c in coef[-2::-1]:
        value = value * z + c
    return value


def split3(value):
    high = value.astype(jnp.bfloat16).astype(jnp.float32)
    rest = value - high
    mid = rest.astype(jnp.bfloat16).astype(jnp.float32)
    return high, mid, rest - mid


def payload_kernel(factor_ref, points_ref, weight_ref, basis_ref, span_ref, patch_ref, cweight_ref, coef_ref, out_ref):
    rounds = points_ref.shape[0]
    controls = cweight_ref.shape[1]
    count = points_ref.shape[2]
    label = lax.broadcasted_iota(jnp.int32, (controls, count), 0)
    pieces = []
    for s in range(rounds):
        span = span_ref[s : s + 1, :]
        patch = patch_ref[s : s + 1, :]
        column = jnp.transpose(jnp.broadcast_to(cweight_ref[s : s + 1, :], (8, controls)))[:, 0:1]
        scaled = []
        for a in range(3):
            picked = jnp.where(label == span + a, column, 0.0)
            scaled.append(basis_ref[s, a : a + 1, :] * jnp.sum(picked, axis=0, keepdims=True))
        denom = scaled[0] + scaled[1] + scaled[2]
        fre = jnp.zeros((1, count), jnp.float32)
        fim = jnp.zeros((1, count), jnp.float32)
        for p in range(factor_ref.shape[2]):
            fre = jnp.where(patch == p, factor_ref[s, 0, p], fre)
            fim = jnp.where(patch == p, factor_ref[s, 1, p], fim)
        weight = weight_ref[s : s + 1, :] / denom
        terms = [value * (weight * fre) for value in scaled] + [value * (weight * fim) for value in scaled]
        high = [t.astype(jnp.bfloat16).astype(jnp.float32) for t in terms]
        low = [t - h for t, h in zip(terms, high)]
        rows = [points_ref[s].astype(jnp.float32), span.astype(jnp.float32)] + high + low
        pieces.append(jnp.concatenate(rows, axis=0))
    coef = jnp.concatenate([jnp.transpose(coef_ref[s].astype(jnp.float32)) for s in range(rounds)], axis=0)
    whole = jnp.concatenate([coef] + pieces, axis=0).astype(jnp.bfloat16)
    for copy in range(out_ref.shape[0]):
        out_ref[copy] = whole


def source_payload(copies, factor, points, weight, basis, span, patch, cweight, coef):
    rounds, fields, controls = coef.shape
    count = points.shape[2]
    rows = rounds * controls + 16 * rounds
    vmem = pl.BlockSpec(memory_space=pltpu.VMEM)
    return pl.pallas_call(
        payload_kernel,
        in_specs=[pl.BlockSpec(memory_space=pltpu.SMEM)] + [vmem] * 7,
        out_specs=vmem,
        out_shape=jax.ShapeDtypeStruct((copies, rows, count), jnp.bfloat16),
        name="payload",
    )(factor, points, weight, basis, span, patch, cweight, coef)


def density_kernel(rounds, controls, gathered_ref, density_ref, feature_ref):
    count = gathered_ref.shape[2]
    base = rounds * controls
    label = lax.broadcasted_iota(jnp.int32, (controls, count), 0).astype(jnp.float32)
    ones = jnp.ones((3, count), jnp.float32)
    zero = jnp.zeros((1, count), jnp.float32)
    for z in range(gathered_ref.shape[0]):
        for s in range(rounds):
            block = z * rounds + s
            rows = gathered_ref[z, base + 16 * s : base + 16 * s + 16, :].astype(jnp.float32)
            pos, span = rows[0:3], rows[3:4]
            masks = [label == span + float(a) for a in range(3)]
            spread = []
            for part in range(4):
                value = jnp.zeros((controls, count), jnp.float32)
                for a in range(3):
                    row = rows[4 + 3 * part + a : 5 + 3 * part + a]
                    value = jnp.where(masks[a], row, value)
                spread.append(value)
            spread = jnp.concatenate(spread, axis=0).astype(jnp.bfloat16)
            plain = gathered_ref[z, s * controls : (s + 1) * controls, :]
            half = plain.shape[1] // 2
            turned = jnp.concatenate([-plain[:, half:], plain[:, :half]], axis=1)
            matrix = jnp.concatenate([plain, turned, plain, turned], axis=0)
            value = lax.dot_general(
                spread, matrix, (((0,), (0,)), ((), ())), preferred_element_type=jnp.float32
            )
            density_ref[block * count : (block + 1) * count, :] = value.astype(jnp.bfloat16)
            norm = pos[0:1] * pos[0:1] + pos[1:2] * pos[1:2] + pos[2:3] * pos[2:3]
            feature = jnp.concatenate([pos, pos, pos, ones, *split3(norm * TURN_SQ), zero], axis=0)
            feature_ref[:, block * count : (block + 1) * count] = feature.astype(jnp.bfloat16)


def source_density(gathered, rounds, controls):
    total = gathered.shape[0] * rounds * gathered.shape[2]
    vmem = pl.BlockSpec(memory_space=pltpu.VMEM)
    return pl.pallas_call(
        functools.partial(density_kernel, rounds, controls),
        in_specs=[vmem],
        out_specs=[vmem, vmem],
        out_shape=[
            jax.ShapeDtypeStruct((total, gathered.shape[2]), jnp.bfloat16),
            jax.ShapeDtypeStruct((16, total), jnp.bfloat16),
        ],
        name="density",
    )(gathered)


def terms_kernel(width, has_start, *refs):
    if has_start:
        target_ref, feature_ref, density_ref, start_ref, out_ref, side_ref, total_ref = refs
    else:
        target_ref, feature_ref, density_ref, out_ref, side_ref, total_ref = refs
    rows = out_ref.shape[0]
    step = pl.program_id(0)

    @pl.when(step == 0)
    def _():
        pos = target_ref[...]
        norm = pos[0:1] * pos[0:1] + pos[1:2] * pos[1:2] + pos[2:3] * pos[2:3] + SMOOTH
        scaled = [p for t in [split3(pos[0:3] * (-2.0 * TURN_SQ))] for p in t]
        ones = jnp.ones((3, pos.shape[1]), jnp.float32)
        side = jnp.concatenate(scaled + [*split3(norm * TURN_SQ), ones, jnp.zeros_like(norm)], axis=0)
        side_ref[...] = jnp.transpose(side)[:rows].astype(jnp.bfloat16)
        total_ref[...] = jnp.zeros_like(total_ref)

    side = side_ref[...]
    chunks = feature_ref.shape[1] // width

    def squared(q):
        return jnp.dot(side, feature_ref[:, q * width : (q + 1) * width], preferred_element_type=jnp.float32)

    def add(terms, q):
        total_ref[...] += jnp.dot(
            terms, density_ref[q * width : (q + 1) * width, :], preferred_element_type=jnp.float32
        )

    square = squared(0)
    ready = None
    for q in range(chunks):
        later = squared(q + 1) if q + 1 < chunks else None
        inverse = lax.rsqrt(square)
        turns = square * inverse
        part = turns - jnp.round(turns)
        z = part * part
        sine = part * horner(z, SIN_POLY)
        cosine = horner(z, COS_POLY)
        scaled = sine * inverse
        kre = (inverse - sine * scaled).astype(jnp.bfloat16)
        kim = (scaled * cosine).astype(jnp.bfloat16)
        terms = jnp.concatenate([kre, kim], axis=0)
        if ready is not None:
            add(ready, q - 1)
        ready, square = terms, later
    add(ready, chunks - 1)

    @pl.when(step == pl.num_programs(0) - 1)
    def _():
        plain = total_ref[:rows]
        other = total_ref[rows:]
        half = plain.shape[1] // 2
        out = plain + jnp.concatenate([-other[:, half:], other[:, :half]], axis=1)
        if has_start:
            out = out + start_ref[...]
        out_ref[...] = out


def kernel_sums(targets, rows, feature, density, start=None, step=1024, width=512):
    total, columns = density.shape
    whole = pl.BlockSpec((rows, columns), lambda i: (0, 0))
    in_specs = [
        pl.BlockSpec(targets.shape, lambda i: (0, 0)),
        pl.BlockSpec((16, step), lambda i: (0, i)),
        pl.BlockSpec((step, columns), lambda i: (i, 0)),
    ]
    args = [targets, feature, density]
    if start is not None:
        in_specs.append(whole)
        args.append(start)
    return pl.pallas_call(
        functools.partial(terms_kernel, width, start is not None),
        grid=(total // step,),
        in_specs=in_specs,
        out_specs=whole,
        out_shape=jax.ShapeDtypeStruct((rows, columns), jnp.float32),
        scratch_shapes=[pltpu.VMEM((rows, 16), jnp.bfloat16), pltpu.VMEM((2 * rows, columns), jnp.float32)],
        compiler_params=pltpu.CompilerParams(vmem_limit_bytes=40 << 20),
        cost_estimate=pl.CostEstimate(
            flops=rows * total * columns * 8, bytes_accessed=total * columns * 2, transcendentals=rows * total
        ),
        name="terms",
    )(*args)


def per_device(
    tgt_points, tgt_weight, src_points, src_weight, basis, span, patch, patch_factor, ctrl_weight, ctrl_coef, band, offsets
):
    rows = tgt_points.shape[1]
    rounds, columns, controls = ctrl_coef.shape
    zs = lax.axis_size("z")
    groups = lax.axis_size(SRC)
    blocks = lax.axis_size(TGT)

    w_high = lax.reduce_precision(tgt_weight, 8, 7)
    w_mid = lax.reduce_precision(tgt_weight - w_high, 8, 7)
    w_rows = jnp.stack([w_high, w_mid, tgt_weight - w_high - w_mid])
    side = jnp.concatenate([tgt_points, w_rows.astype(jnp.bfloat16), jnp.zeros((2, rows), jnp.bfloat16)], axis=0)
    forward = [(i, i + 1) for i in range(blocks - 1)]
    low = lax.ppermute(side, TGT, forward)
    high = lax.ppermute(side, TGT, [(b, a) for a, b in forward])
    span_rows = rows + 2 * HALO
    lanes = -(-span_rows // 128) * 128
    wide = jnp.concatenate(
        [low[:, rows - HALO :], side, high[:, :HALO], jnp.zeros((8, lanes - span_rows), jnp.bfloat16)], axis=1
    )
    swap = [(0, 1), (1, 0)]
    wide_peer = lax.ppermute(wide, "yh", swap)
    own_pos = wide.astype(jnp.float32)
    peer_pos = wide_peer.astype(jnp.float32)

    sent = source_payload(
        zs, patch_factor, src_points, src_weight, basis, span, patch, ctrl_weight, ctrl_coef
    )
    gathered = lax.all_to_all(sent, "z", split_axis=0, concat_axis=0, tiled=True)
    density, feature = source_density(gathered, rounds, controls)
    density2 = lax.ppermute(density, "core", swap)
    feature2 = lax.ppermute(feature, "core", swap)

    peer = kernel_sums(peer_pos, span_rows, feature, density)
    peer = kernel_sums(peer_pos, span_rows, feature2, density2, peer)
    arrived = lax.ppermute(peer, "yh", swap)
    own = kernel_sums(own_pos, span_rows, feature, density)
    own = kernel_sums(own_pos, span_rows, feature2, density2, own)
    own = own + arrived

    share = -(-span_rows // (8 * groups)) * 8
    own = jnp.pad(own, ((0, share * groups - span_rows), (0, 0))).reshape(groups, share, columns)
    shares = lax.all_to_all(own, SRC, split_axis=0, concat_axis=0, tiled=True)
    summed = jnp.sum(shares, axis=0)
    spread = jnp.broadcast_to(summed[None], (groups, share, columns))
    total = lax.all_to_all(spread, SRC, split_axis=0, concat_axis=0, tiled=True)
    total = total.reshape(groups * share, columns)[:span_rows]

    source_count = rounds * src_weight.shape[1] * blocks * groups
    scale = jnp.float32(TURN / math.sqrt(source_count))
    tail = own_pos[3:6, :span_rows]
    weight = (tail[0] + tail[1]) + tail[2]
    padded = total * (weight * scale)[:, None]
    potential = lax.slice_in_dim(padded, HALO, HALO + rows, axis=0)
    shell_field = potential
    for diag in range(band.shape[0]):
        shifted = lax.dynamic_slice_in_dim(padded, HALO + offsets[diag], rows, 0)
        shell_field = shell_field + band[diag][:, None] * shifted
    return shell_field


def solution(mesh):
    mesh = Mesh(mesh.devices.reshape(8, 2, 2, 2, 4), ("z", "yh", "core", "yl", "x"))
    both = TGT + SRC
    in_specs = (
        P(None, TGT),
        P(TGT),
        P(None, None, both),
        P(None, both),
        P(None, None, both),
        P(None, both),
        P(None, both),
        P(None, None, both),
        P(None, both),
        P(None, None, both),
        P(None, TGT),
        P(),
    )
    return jax.shard_map(
        per_device, mesh=mesh, in_specs=in_specs, out_specs=P(TGT, None), check_vma=False
    )
```

```python
import functools
import math

import jax
import jax.numpy as jnp
import numpy as np
from jax import lax
from jax.experimental import pallas as pl
from jax.experimental.pallas import tpu as pltpu
from jax.sharding import Mesh, PartitionSpec as P

HALO = 8
WAVE = 8.0
SMOOTH = 0.0025
TURN = WAVE / (2.0 * math.pi)
TURN_SQ = TURN * TURN

TGT = ("z", "yh", "core")
SRC = ("yl", "x")


def minimax(func, importance, terms, odd):
    nodes = 0.25 + 0.25 * np.cos(np.linspace(0.0, np.pi, 2001))
    nodes = nodes[nodes > 1e-6]
    scale = nodes if odd else np.ones_like(nodes)
    matter = importance(nodes)
    basis = np.stack([nodes ** (2 * k) for k in range(terms)], 1)
    value = func(nodes) / scale
    weight = np.ones_like(nodes)
    for _ in range(60):
        rows = scale * weight * matter
        coef = np.linalg.lstsq(basis * rows[:, None], value * rows, rcond=None)[0]
        error = np.abs((basis @ coef - value) * scale * matter)
        weight = weight * np.sqrt(1e-12 + error / error.max())
        weight = weight / weight.mean()
    return tuple(float(np.float32(c)) for c in coef)


SIN_POLY = minimax(lambda f: math.sqrt(2.0) * np.sin(np.pi * f), np.ones_like, 3, True)
COS_POLY = minimax(lambda f: math.sqrt(2.0) * np.cos(np.pi * f), lambda f: np.sin(np.pi * f), 3, False)
COS_LEAD = COS_POLY[-1]
COS_MONIC = tuple(c / COS_LEAD for c in COS_POLY[:-1]) + (1.0,)


def horner(z, coef):
    value = z + coef[-2] if coef[-1] == 1.0 else coef[-1] * z + coef[-2]
    for c in coef[-3::-1]:
        value = value * z + c
    return value


def split3(value):
    high = value.astype(jnp.bfloat16).astype(jnp.float32)
    rest = value - high
    mid = rest.astype(jnp.bfloat16).astype(jnp.float32)
    return high, mid, rest - mid


def payload_kernel(factor_ref, points_ref, weight_ref, basis_ref, span_ref, patch_ref, cweight_ref, coef_ref, target_ref, tweight_ref, out_ref, side_ref):
    rounds, controls = cweight_ref.shape
    count = points_ref.shape[2]
    label = lax.broadcasted_iota(jnp.int32, (controls, count), 0)
    pieces = []
    for s in range(rounds):
        span = span_ref[s : s + 1, :]
        patch = patch_ref[s : s + 1, :]
        column = jnp.transpose(jnp.broadcast_to(cweight_ref[s : s + 1, :], (8, controls)))[:, 0:1]
        scaled = []
        for a in range(3):
            picked = jnp.where(label == span + a, column, 0.0)
            scaled.append(basis_ref[a, s : s + 1, :] * jnp.sum(picked, axis=0, keepdims=True))
        denom = scaled[0] + scaled[1] + scaled[2]
        fre = jnp.zeros((1, count), jnp.float32)
        fim = jnp.zeros((1, count), jnp.float32)
        for p in range(factor_ref.shape[2]):
            fre = jnp.where(patch == p, factor_ref[s, 0, p], fre)
            fim = jnp.where(patch == p, factor_ref[s, 1, p], fim)
        weight = weight_ref[s : s + 1, :] / denom
        terms = [value * (weight * fre) for value in scaled] + [value * (weight * fim) for value in scaled]
        high = [t.astype(jnp.bfloat16).astype(jnp.float32) for t in terms]
        low = [t - h for t, h in zip(terms, high)]
        rows = [points_ref[c, s : s + 1, :].astype(jnp.float32) for c in range(3)] + [span.astype(jnp.float32)] + high + low
        pieces.append(jnp.concatenate(rows, axis=0))
    extra = jnp.concatenate(pieces, axis=0).astype(jnp.bfloat16)
    for copy in range(out_ref.shape[0]):
        out_ref[copy, : rounds * controls, :] = coef_ref[...]
        out_ref[copy, rounds * controls :, :] = extra
    parts = [target_ref[...].astype(jnp.float32), *split3(tweight_ref[...])]
    zero = jnp.zeros((2, target_ref.shape[1]), jnp.float32)
    side_ref[...] = jnp.concatenate(parts + [zero], axis=0).astype(jnp.bfloat16)


def source_payload(copies, factor, points, weight, basis, span, patch, cweight, coef, target, tweight):
    rounds, fields, controls = coef.shape
    count = points.shape[2]
    rows = rounds * controls + 16 * rounds
    points = jnp.transpose(points, (1, 0, 2))
    basis = jnp.transpose(basis, (1, 0, 2))
    coef = jnp.transpose(coef, (0, 2, 1)).reshape(rounds * controls, fields)
    vmem = pl.BlockSpec(memory_space=pltpu.VMEM)
    return pl.pallas_call(
        payload_kernel,
        in_specs=[pl.BlockSpec(memory_space=pltpu.SMEM)] + [vmem] * 9,
        out_specs=[vmem, vmem],
        out_shape=[
            jax.ShapeDtypeStruct((copies, rows, count), jnp.bfloat16),
            jax.ShapeDtypeStruct((8, target.shape[1]), jnp.bfloat16),
        ],
        name="payload",
    )(factor, points, weight, basis, span, patch, cweight, coef, target, tweight.reshape(1, -1))


def source_rows(gathered_ref, q, s, rounds, controls):
    first = rounds * controls + 16 * s
    return gathered_ref[q, first : first + 16, :].astype(jnp.float32)


def source_features(gathered_ref, q, rounds, controls):
    pieces = []
    for s in range(rounds):
        pos = source_rows(gathered_ref, q, s, rounds, controls)[0:3]
        norm = pos[0:1] * pos[0:1] + pos[1:2] * pos[1:2] + pos[2:3] * pos[2:3]
        parts = [pos, pos, pos, jnp.ones_like(pos), *split3(norm * TURN_SQ), jnp.zeros_like(norm)]
        pieces.append(jnp.concatenate(parts, axis=0).astype(jnp.bfloat16))
    return jnp.concatenate(pieces, axis=1)


def source_density(gathered_ref, q, rounds, controls):
    count = gathered_ref.shape[2]
    label = lax.broadcasted_iota(jnp.int32, (controls, count), 0).astype(jnp.float32)
    pieces = []
    for s in range(rounds):
        rows = source_rows(gathered_ref, q, s, rounds, controls)
        masks = [label == rows[3:4] + float(a) for a in range(3)]
        spread = []
        for part in range(4):
            value = jnp.zeros((controls, count), jnp.float32)
            for a in range(3):
                value = jnp.where(masks[a], rows[4 + 3 * part + a : 5 + 3 * part + a], value)
            spread.append(value)
        spread = jnp.concatenate(spread, axis=0).astype(jnp.bfloat16)
        plain = gathered_ref[q, s * controls : (s + 1) * controls, :]
        half = plain.shape[1] // 2
        turned = jnp.concatenate([-plain[:, half:], plain[:, :half]], axis=1)
        matrix = jnp.concatenate([plain, turned, plain, turned], axis=0)
        value = lax.dot_general(spread, matrix, (((0,), (0,)), ((), ())), preferred_element_type=jnp.float32)
        pieces.append(value.astype(jnp.bfloat16))
    return jnp.concatenate(pieces, axis=0)


def target_features(target_ref, rows):
    pos = target_ref[...].astype(jnp.float32)
    norm = pos[0:1] * pos[0:1] + pos[1:2] * pos[1:2] + pos[2:3] * pos[2:3] + SMOOTH
    scaled = [*split3(pos[0:3] * (-2.0 * TURN_SQ))]
    ones = jnp.ones((3, pos.shape[1]), jnp.float32)
    side = jnp.concatenate(scaled + [*split3(norm * TURN_SQ), ones, jnp.zeros_like(norm)], axis=0)
    return jnp.transpose(side)[:rows].astype(jnp.bfloat16)


def kernel_terms(square):
    inverse = lax.rsqrt(square)
    turns = square * inverse
    part = turns - jnp.round(turns)
    z = part * part
    sine = part * horner(z, SIN_POLY)
    cosine = horner(z, COS_MONIC)
    scaled = sine * inverse
    kre = (inverse - sine * scaled).astype(jnp.bfloat16)
    kim = (scaled * cosine).astype(jnp.bfloat16)
    return jnp.concatenate([kre, kim], axis=0)


def terms_kernel(make, rounds, controls, has_start, *refs):
    refs = list(refs)
    target_ref = refs.pop(0)
    gathered_ref = refs.pop(0) if make else None
    density_in, feature_in = (None, None) if make else (refs.pop(0), refs.pop(0))
    start_ref = refs.pop(0) if has_start else None
    out_ref = refs.pop(0)
    density_out, feature_out = (refs.pop(0), refs.pop(0)) if make else (None, None)
    side_ref, total_ref = refs
    rows, columns = out_ref.shape
    step = pl.program_id(0)

    @pl.when(step == 0)
    def _():
        side_ref[...] = target_features(target_ref, rows)
        total_ref[...] = jnp.zeros_like(total_ref)

    side = side_ref[...]
    if make:
        chunks, width = gathered_ref.shape[0], rounds * gathered_ref.shape[2]
    else:
        width = 512
        chunks = density_in.shape[0] // width

    def squared(q):
        if make:
            feature = source_features(gathered_ref, q, rounds, controls)
            feature_out[:, q * width : (q + 1) * width] = feature
        else:
            feature = feature_in[:, q * width : (q + 1) * width]
        return jnp.dot(side, feature, preferred_element_type=jnp.float32)

    def densities(q):
        if make:
            density = source_density(gathered_ref, q, rounds, controls)
            density_out[q * width : (q + 1) * width, :] = density
            return density
        return density_in[q * width : (q + 1) * width, :]

    def add(terms, density):
        total_ref[...] += jnp.dot(terms, density, preferred_element_type=jnp.float32)

    square = squared(0)
    ready = None
    for q in range(chunks):
        later = squared(q + 1) if q + 1 < chunks else None
        density = densities(q)
        terms = kernel_terms(square)
        if ready is not None:
            add(*ready)
        ready, square = (terms, density), later
    add(*ready)

    @pl.when(step == pl.num_programs(0) - 1)
    def _():
        plain = total_ref[:rows]
        other = total_ref[rows:] * COS_LEAD
        half = columns // 2
        out = plain + jnp.concatenate([-other[:, half:], other[:, :half]], axis=1)
        if has_start:
            out = out + start_ref[...]
        out_ref[...] = out


def kernel_sums(targets, rows, columns, sources, rounds, controls, start=None):
    make = not isinstance(sources, tuple)
    whole = pl.BlockSpec((rows, columns), lambda i: (0, 0))
    step = 2048
    if make:
        groups, depth, count = sources.shape
        total = groups * rounds * count
        per_step = step // (rounds * count)
        source_specs = [pl.BlockSpec((per_step, depth, count), lambda i: (i, 0, 0))]
        sources = (sources,)
    else:
        total = sources[0].shape[0]
        source_specs = []
    ready_specs = [pl.BlockSpec((step, columns), lambda i: (i, 0)), pl.BlockSpec((16, step), lambda i: (0, i))]
    sums = jax.ShapeDtypeStruct((rows, columns), jnp.float32)
    ready = [
        jax.ShapeDtypeStruct((total, columns), jnp.bfloat16),
        jax.ShapeDtypeStruct((16, total), jnp.bfloat16),
    ]
    in_specs = [pl.BlockSpec(targets.shape, lambda i: (0, 0))] + (source_specs if make else ready_specs)
    args = [targets, *sources]
    if start is not None:
        in_specs.append(whole)
        args.append(start)
    return pl.pallas_call(
        functools.partial(terms_kernel, make, rounds, controls, start is not None),
        grid=(total // step,),
        in_specs=in_specs,
        out_specs=[whole] + ready_specs if make else whole,
        out_shape=[sums] + ready if make else sums,
        scratch_shapes=[pltpu.VMEM((rows, 16), jnp.bfloat16), pltpu.VMEM((2 * rows, columns), jnp.float32)],
        compiler_params=pltpu.CompilerParams(vmem_limit_bytes=24 << 20),
        cost_estimate=pl.CostEstimate(
            flops=rows * total * columns * 8, bytes_accessed=total * columns * 2, transcendentals=rows * total
        ),
        name="terms",
    )(*args)


def band_kernel(scale, offsets_ref, own_ref, side_ref, band_ref, out_ref, pot_ref):
    rows = own_ref.shape[0]
    columns = own_ref.shape[1]
    block = band_ref.shape[1]
    side = side_ref[...].astype(jnp.float32)
    weight = (side[3:4] + side[4:5]) + side[5:6]
    weight = jnp.transpose(jnp.broadcast_to(weight * scale, (8, weight.shape[1])))[:rows, 0:1]
    pot_ref[...] = own_ref[...] * weight
    factors = jnp.transpose(band_ref[...])
    shell = pot_ref[HALO : HALO + block, :]
    for diag in range(band_ref.shape[0]):
        shifted = pot_ref[pl.ds(HALO + offsets_ref[diag], block), :]
        shell = shell + factors[:, diag : diag + 1] * shifted
    shell = shell.astype(jnp.bfloat16)
    for copy in range(out_ref.shape[0]):
        out_ref[copy] = shell


def band_shares(copies, scale, offsets, own, side, band):
    vmem = pl.BlockSpec(memory_space=pltpu.VMEM)
    block, columns = band.shape[1], own.shape[1]
    return pl.pallas_call(
        functools.partial(band_kernel, scale),
        in_specs=[pl.BlockSpec(memory_space=pltpu.SMEM)] + [vmem] * 3,
        out_specs=vmem,
        out_shape=jax.ShapeDtypeStruct((copies, block, columns), jnp.bfloat16),
        scratch_shapes=[pltpu.VMEM(own.shape, jnp.float32)],
        compiler_params=pltpu.CompilerParams(vmem_limit_bytes=16 << 20),
        name="band",
    )(offsets, own, side, band)


def per_device(
    tgt_points, tgt_weight, src_points, src_weight, basis, span, patch, patch_factor, ctrl_weight, ctrl_coef, band, offsets
):
    rows = tgt_points.shape[1]
    rounds, columns, controls = ctrl_coef.shape
    zs = lax.axis_size("z")
    groups = lax.axis_size(SRC)
    blocks = lax.axis_size(TGT)
    swap = [(0, 1), (1, 0)]

    sent, side = source_payload(
        zs, patch_factor, src_points, src_weight, basis, span, patch, ctrl_weight, ctrl_coef, tgt_points, tgt_weight
    )
    partner = lax.ppermute(side, "core", swap)
    links = [(k, k + 1) for k in range(1, blocks - 1, 2)]
    across = lax.ppermute(side, TGT, links + [(b, a) for a, b in links])
    gathered = lax.all_to_all(sent, "z", split_axis=0, concat_axis=0, tiled=True)

    first = lax.axis_index("core") == 0
    span_rows = rows + 2 * HALO
    lanes = -(-span_rows // 128) * 128
    low = jnp.where(first, across, partner)[:, rows - HALO :]
    high = jnp.where(first, partner, across)[:, :HALO]
    wide = jnp.concatenate([low, side, high, jnp.zeros((8, lanes - span_rows), jnp.bfloat16)], axis=1)

    gathered2 = lax.ppermute(gathered, "yh", swap)
    sums, *made = kernel_sums(wide, span_rows, columns, gathered, rounds, controls)
    made = tuple(lax.ppermute(part, "core", swap) for part in made)
    sums, *made2 = kernel_sums(wide, span_rows, columns, gathered2, rounds, controls, sums)
    made2 = tuple(lax.ppermute(part, "core", swap) for part in made2)
    sums = kernel_sums(wide, span_rows, columns, made, rounds, controls, sums)
    sums = kernel_sums(wide, span_rows, columns, made2, rounds, controls, sums)

    source_count = rounds * src_weight.shape[1] * blocks * groups
    scale = TURN / math.sqrt(source_count)
    shares = band_shares(groups, scale, offsets, sums, wide, band)
    shares = lax.all_to_all(shares, SRC, split_axis=0, concat_axis=0, tiled=True)
    return jnp.sum(shares.astype(jnp.float32), axis=0)


def solution(mesh):
    mesh = Mesh(mesh.devices.reshape(8, 2, 2, 2, 4), ("z", "yh", "core", "yl", "x"))
    both = TGT + SRC
    in_specs = (
        P(None, TGT),
        P(TGT),
        P(None, None, both),
        P(None, both),
        P(None, None, both),
        P(None, both),
        P(None, both),
        P(None, None, both),
        P(None, both),
        P(None, None, both),
        P(None, TGT),
        P(),
    )
    return jax.shard_map(
        per_device, mesh=mesh, in_specs=in_specs, out_specs=P(TGT, None), check_vma=False
    )
```

```python
import functools
import math

import jax
import jax.numpy as jnp
import numpy as np
from jax import lax
from jax.experimental import pallas as pl
from jax.experimental.pallas import tpu as pltpu
from jax.sharding import Mesh, PartitionSpec as P

HALO = 8
WAVE = 8.0
SMOOTH = 0.0025
TURN = WAVE / (2.0 * math.pi)
TURN_SQ = TURN * TURN

TGT = ("z", "yh", "core")
SRC = ("yl", "x")


def minimax(func, importance, terms, odd):
    nodes = 0.25 + 0.25 * np.cos(np.linspace(0.0, np.pi, 2001))
    nodes = nodes[nodes > 1e-6]
    scale = nodes if odd else np.ones_like(nodes)
    matter = importance(nodes)
    basis = np.stack([nodes ** (2 * k) for k in range(terms)], 1)
    value = func(nodes) / scale
    weight = np.ones_like(nodes)
    for _ in range(60):
        rows = scale * weight * matter
        coef = np.linalg.lstsq(basis * rows[:, None], value * rows, rcond=None)[0]
        error = np.abs((basis @ coef - value) * scale * matter)
        weight = weight * np.sqrt(1e-12 + error / error.max())
        weight = weight / weight.mean()
    return tuple(float(np.float32(c)) for c in coef)


SIN_POLY = minimax(lambda f: math.sqrt(2.0) * np.sin(np.pi * f), np.ones_like, 3, True)
COS_POLY = minimax(lambda f: math.sqrt(2.0) * np.cos(np.pi * f), lambda f: np.sin(np.pi * f), 3, False)
COS_LEAD = COS_POLY[-1]
COS_MONIC = tuple(c / COS_LEAD for c in COS_POLY[:-1]) + (1.0,)


def horner(z, coef):
    value = z + coef[-2] if coef[-1] == 1.0 else coef[-1] * z + coef[-2]
    for c in coef[-3::-1]:
        value = value * z + c
    return value


def split3(value):
    high = value.astype(jnp.bfloat16).astype(jnp.float32)
    rest = value - high
    mid = rest.astype(jnp.bfloat16).astype(jnp.float32)
    return high, mid, rest - mid


def payload_kernel(factor_ref, points_ref, weight_ref, basis_ref, span_ref, patch_ref, cweight_ref, coef_ref, target_ref, tweight_ref, out_ref, side_ref):
    rounds, controls = cweight_ref.shape
    count = points_ref.shape[2]
    label = lax.broadcasted_iota(jnp.int32, (controls, count), 0)
    pieces = []
    for s in range(rounds):
        span = span_ref[s : s + 1, :]
        patch = patch_ref[s : s + 1, :]
        column = jnp.transpose(jnp.broadcast_to(cweight_ref[s : s + 1, :], (8, controls)))[:, 0:1]
        scaled = []
        for a in range(3):
            picked = jnp.where(label == span + a, column, 0.0)
            scaled.append(basis_ref[a, s : s + 1, :] * jnp.sum(picked, axis=0, keepdims=True))
        denom = scaled[0] + scaled[1] + scaled[2]
        fre = jnp.zeros((1, count), jnp.float32)
        fim = jnp.zeros((1, count), jnp.float32)
        for p in range(factor_ref.shape[2]):
            fre = jnp.where(patch == p, factor_ref[s, 0, p], fre)
            fim = jnp.where(patch == p, factor_ref[s, 1, p], fim)
        weight = weight_ref[s : s + 1, :] / denom
        terms = [value * (weight * fre) for value in scaled] + [value * (weight * fim) for value in scaled]
        high = [t.astype(jnp.bfloat16).astype(jnp.float32) for t in terms]
        low = [t - h for t, h in zip(terms, high)]
        rows = [points_ref[c, s : s + 1, :].astype(jnp.float32) for c in range(3)] + [span.astype(jnp.float32)] + high + low
        pieces.append(jnp.concatenate(rows, axis=0))
    extra = jnp.concatenate(pieces, axis=0).astype(jnp.bfloat16)
    for copy in range(out_ref.shape[0]):
        out_ref[copy, : rounds * controls, :] = coef_ref[...]
        out_ref[copy, rounds * controls :, :] = extra
    parts = [target_ref[...].astype(jnp.float32), *split3(tweight_ref[...])]
    zero = jnp.zeros((2, target_ref.shape[1]), jnp.float32)
    side_ref[...] = jnp.concatenate(parts + [zero], axis=0).astype(jnp.bfloat16)


def source_payload(copies, factor, points, weight, basis, span, patch, cweight, coef, target, tweight):
    rounds, fields, controls = coef.shape
    count = points.shape[2]
    rows = rounds * controls + 16 * rounds
    points = jnp.transpose(points, (1, 0, 2))
    basis = jnp.transpose(basis, (1, 0, 2))
    coef = jnp.transpose(coef, (0, 2, 1)).reshape(rounds * controls, fields)
    vmem = pl.BlockSpec(memory_space=pltpu.VMEM)
    return pl.pallas_call(
        payload_kernel,
        in_specs=[pl.BlockSpec(memory_space=pltpu.SMEM)] + [vmem] * 9,
        out_specs=[vmem, vmem],
        out_shape=[
            jax.ShapeDtypeStruct((copies, rows, count), jnp.bfloat16),
            jax.ShapeDtypeStruct((8, target.shape[1]), jnp.bfloat16),
        ],
        name="payload",
    )(factor, points, weight, basis, span, patch, cweight, coef, target, tweight.reshape(1, -1))


def source_rows(gathered_ref, q, s, rounds, controls):
    first = rounds * controls + 16 * s
    return gathered_ref[q, first : first + 16, :].astype(jnp.float32)


def source_features(gathered_ref, q, rounds, controls):
    pieces = []
    for s in range(rounds):
        pos = source_rows(gathered_ref, q, s, rounds, controls)[0:3]
        norm = pos[0:1] * pos[0:1] + pos[1:2] * pos[1:2] + pos[2:3] * pos[2:3]
        parts = [pos, pos, pos, jnp.ones_like(pos), *split3(norm * TURN_SQ), jnp.zeros_like(norm)]
        pieces.append(jnp.concatenate(parts, axis=0).astype(jnp.bfloat16))
    return pieces


def source_density(gathered_ref, q, rounds, controls):
    count = gathered_ref.shape[2]
    label = lax.broadcasted_iota(jnp.int32, (controls, count), 0).astype(jnp.float32)
    pieces = []
    for s in range(rounds):
        rows = source_rows(gathered_ref, q, s, rounds, controls)
        masks = [label == rows[3:4] + float(a) for a in range(3)]
        spread = []
        for part in range(4):
            value = jnp.zeros((controls, count), jnp.float32)
            for a in range(3):
                value = jnp.where(masks[a], rows[4 + 3 * part + a : 5 + 3 * part + a], value)
            spread.append(value)
        spread = jnp.concatenate(spread, axis=0).astype(jnp.bfloat16)
        plain = gathered_ref[q, s * controls : (s + 1) * controls, :]
        half = plain.shape[1] // 2
        turned = jnp.concatenate([-plain[:, half:], plain[:, :half]], axis=1)
        matrix = jnp.concatenate([plain, turned, plain, turned], axis=0)
        value = lax.dot_general(spread, matrix, (((0,), (0,)), ((), ())), preferred_element_type=jnp.float32)
        pieces.append(value.astype(jnp.bfloat16))
    return jnp.concatenate(pieces, axis=0)


def widened(low, middle, high, rows, lanes):
    count = middle.shape[1]
    place = lax.broadcasted_iota(jnp.int32, (8, lanes), 1)

    def moved(value, shift):
        pad = jnp.concatenate([value, jnp.zeros((8, lanes - count), jnp.float32)], axis=1)
        return pltpu.roll(pad, shift % lanes, 1)

    inner = jnp.where(place < HALO + count, moved(middle, HALO), moved(high, HALO + count))
    outer = jnp.where(place < HALO, moved(low, HALO - count), inner)
    return jnp.where(place < rows, outer, 0.0)


def target_features(pos, rows):
    norm = pos[0:1] * pos[0:1] + pos[1:2] * pos[1:2] + pos[2:3] * pos[2:3] + SMOOTH
    scaled = [*split3(pos[0:3] * (-2.0 * TURN_SQ))]
    ones = jnp.ones((3, pos.shape[1]), jnp.float32)
    side = jnp.concatenate(scaled + [*split3(norm * TURN_SQ), ones, jnp.zeros_like(norm)], axis=0)
    return jnp.transpose(side)[:rows].astype(jnp.bfloat16)


def kernel_terms(square):
    inverse = lax.rsqrt(square)
    turns = square * inverse
    part = turns - jnp.round(turns)
    z = part * part
    sine = part * horner(z, SIN_POLY)
    cosine = horner(z, COS_MONIC)
    scaled = sine * inverse
    kre = (inverse - sine * scaled).astype(jnp.bfloat16)
    kim = (scaled * cosine).astype(jnp.bfloat16)
    return jnp.concatenate([kre, kim], axis=0)


def terms_kernel(first, make, rounds, controls, *refs):
    refs = list(refs)
    if first:
        core_ref, block_ref, other_ref, source_ref, out_ref, wide_ref, side_ref, total_ref = refs
        ready_ref = None
    elif make:
        wide_ref, source_ref, start_ref, out_ref, ready_ref, side_ref, total_ref = refs
    else:
        wide_ref, source_ref, start_ref, out_ref, side_ref, total_ref = refs
        ready_ref = source_ref
    tiles, rows, columns = out_ref.shape
    count = source_ref.shape[-1]
    width = rounds * count
    depth = width + 16 * rounds
    chunks = source_ref.shape[0] if make else source_ref.shape[0] // depth
    step = pl.program_id(0)

    @pl.when(step == 0)
    def _():
        if first:
            lanes = wide_ref.shape[2]
            low_core = core_ref[0] == 0
            block, across = block_ref[:8].astype(jnp.float32), block_ref[8:].astype(jnp.float32)
            other, beyond = other_ref[:8].astype(jnp.float32), other_ref[8:].astype(jnp.float32)
            pick = lambda a, b: jnp.where(low_core, a, b)
            wide_ref[0] = widened(pick(across, other), block, pick(other, across), rows, lanes)
            wide_ref[1] = widened(pick(block, beyond), other, pick(beyond, block), rows, lanes)
        for t in range(tiles):
            side_ref[t] = target_features(wide_ref[t], rows)
        total_ref[...] = jnp.zeros_like(total_ref)

    features, densities = {}, {}

    def squared(q, t):
        if q not in features:
            places = [slice(q * depth + width + 16 * s, q * depth + width + 16 * (s + 1)) for s in range(rounds)]
            if make:
                pieces = source_features(source_ref, q, rounds, controls)
                if ready_ref is not None:
                    for place, piece in zip(places, pieces):
                        ready_ref[place, :] = piece
            else:
                pieces = [ready_ref[place, :] for place in places]
            features[q] = jnp.concatenate(pieces, axis=1)
        return jnp.dot(side_ref[t], features[q], preferred_element_type=jnp.float32)

    def density(q):
        if q not in densities:
            place = slice(q * depth, q * depth + width)
            if make:
                densities[q] = source_density(source_ref, q, rounds, controls)
                if ready_ref is not None:
                    ready_ref[place, :] = densities[q]
            else:
                densities[q] = ready_ref[place, :]
        return densities[q]

    def add(terms, q, t):
        total_ref[t] += jnp.dot(terms, density(q), preferred_element_type=jnp.float32)

    items = [(q, t) for q in range(chunks) for t in range(tiles)]
    square = squared(*items[0])
    waiting = None
    for n, (q, t) in enumerate(items):
        later = squared(*items[n + 1]) if n + 1 < len(items) else None
        density(q)
        terms = kernel_terms(square)
        if waiting is not None:
            add(*waiting)
        waiting, square = (terms, q, t), later
    add(*waiting)

    @pl.when(step == pl.num_programs(0) - 1)
    def _():
        for t in range(tiles):
            plain = total_ref[t, :rows]
            other = total_ref[t, rows:] * COS_LEAD
            half = columns // 2
            out = plain + jnp.concatenate([-other[:, half:], other[:, :half]], axis=1)
            if not first:
                out = out + start_ref[t]
            out_ref[t] = out


def kernel_sums(rows, lanes, sources, rounds, controls, make, blocks=None, wide=None, start=None, tile=0):
    first = blocks is not None
    tiles = 2 if first else 1
    count = sources.shape[-1]
    chunk = rounds * count + 16 * rounds
    per_step = 2 if first else 4
    if make:
        chunks = sources.shape[0]
        source_spec = pl.BlockSpec((per_step,) + sources.shape[1:], lambda i: (i, 0, 0))
    else:
        chunks = sources.shape[0] // chunk
        source_spec = pl.BlockSpec((per_step * chunk, count), lambda i: (i, 0))
    out_specs = [pl.BlockSpec((tiles, rows, count), lambda i: (0, 0, 0))]
    out_shape = [jax.ShapeDtypeStruct((tiles, rows, count), jnp.float32)]
    if first:
        core, block, other = blocks
        whole = pl.BlockSpec(block.shape, lambda i: (0, 0))
        in_specs = [pl.BlockSpec(memory_space=pltpu.SMEM), whole, whole, source_spec]
        args = [core, block, other, sources]
        out_specs.append(pl.BlockSpec((2, 8, lanes), lambda i: (0, 0, 0)))
        out_shape.append(jax.ShapeDtypeStruct((2, 8, lanes), jnp.float32))
    else:
        in_specs = [
            pl.BlockSpec((1, 8, lanes), lambda i: (tile, 0, 0)),
            source_spec,
            pl.BlockSpec((1, rows, count), lambda i: (tile, 0, 0)),
        ]
        args = [wide, sources, start]
        if make:
            out_specs.append(pl.BlockSpec((per_step * chunk, count), lambda i: (i, 0)))
            out_shape.append(jax.ShapeDtypeStruct((chunks * chunk, count), jnp.bfloat16))
    pairs = tiles * rows * chunks * rounds * count
    return pl.pallas_call(
        functools.partial(terms_kernel, first, make, rounds, controls),
        grid=(chunks // per_step,),
        in_specs=in_specs,
        out_specs=out_specs,
        out_shape=out_shape,
        scratch_shapes=[
            pltpu.VMEM((tiles, rows, 16), jnp.bfloat16),
            pltpu.VMEM((tiles, 2 * rows, count), jnp.float32),
        ],
        compiler_params=pltpu.CompilerParams(vmem_limit_bytes=24 << 20),
        cost_estimate=pl.CostEstimate(flops=pairs * count * 8, bytes_accessed=1 << 20, transcendentals=pairs),
        name="terms",
    )(*args)


def band_kernel(scale, offsets_ref, own_ref, arrived_ref, side_ref, band_ref, out_ref, pot_ref):
    rows = own_ref.shape[0]
    columns = own_ref.shape[1]
    block = band_ref.shape[1]
    side = side_ref[...]
    weight = (side[3:4] + side[4:5]) + side[5:6]
    weight = jnp.transpose(jnp.broadcast_to(weight * scale, (8, weight.shape[1])))[:rows, 0:1]
    pot_ref[...] = (own_ref[...] + arrived_ref[...]) * weight
    factors = jnp.transpose(band_ref[...])
    shell = pot_ref[HALO : HALO + block, :]
    for diag in range(band_ref.shape[0]):
        shifted = pot_ref[pl.ds(HALO + offsets_ref[diag], block), :]
        shell = shell + factors[:, diag : diag + 1] * shifted
    shell = shell.astype(jnp.bfloat16)
    for copy in range(out_ref.shape[0]):
        out_ref[copy] = shell


def band_shares(copies, scale, offsets, own, arrived, side, band):
    vmem = pl.BlockSpec(memory_space=pltpu.VMEM)
    block, columns = band.shape[1], own.shape[1]
    return pl.pallas_call(
        functools.partial(band_kernel, scale),
        in_specs=[pl.BlockSpec(memory_space=pltpu.SMEM)] + [vmem] * 4,
        out_specs=vmem,
        out_shape=jax.ShapeDtypeStruct((copies, block, columns), jnp.bfloat16),
        scratch_shapes=[pltpu.VMEM(own.shape, jnp.float32)],
        compiler_params=pltpu.CompilerParams(vmem_limit_bytes=16 << 20),
        name="band",
    )(offsets, own, arrived, side, band)


def per_device(
    tgt_points, tgt_weight, src_points, src_weight, basis, span, patch, patch_factor, ctrl_weight, ctrl_coef, band, offsets
):
    rows = tgt_points.shape[1]
    rounds, columns, controls = ctrl_coef.shape
    zs = lax.axis_size("z")
    groups = lax.axis_size(SRC)
    blocks = lax.axis_size(TGT)
    swap = [(0, 1), (1, 0)]

    sent, side = source_payload(
        zs, patch_factor, src_points, src_weight, basis, span, patch, ctrl_weight, ctrl_coef, tgt_points, tgt_weight
    )
    links = [(k, k + 1) for k in range(1, blocks - 1, 2)]
    across = lax.ppermute(side, TGT, links + [(b, a) for a, b in links])
    gathered = lax.all_to_all(sent, "z", split_axis=0, concat_axis=0, tiled=True)
    block = jnp.concatenate([side, across], axis=0)
    other = lax.ppermute(block, "core", swap)
    core = lax.axis_index("core").astype(jnp.int32).reshape(1)

    span_rows = rows + 2 * HALO
    lanes = -(-span_rows // 128) * 128
    gathered2 = lax.ppermute(gathered, "yh", swap)
    shapes = (span_rows, lanes)
    sums, wide = kernel_sums(*shapes, gathered, rounds, controls, True, blocks=(core, block, other))
    share, made = kernel_sums(*shapes, gathered2, rounds, controls, True, wide=wide, start=sums, tile=1)
    arrived = lax.ppermute(share, "core", swap)
    (own,) = kernel_sums(*shapes, made, rounds, controls, False, wide=wide, start=sums, tile=0)

    source_count = rounds * src_weight.shape[1] * blocks * groups
    scale = TURN / math.sqrt(source_count)
    shares = band_shares(groups, scale, offsets, own[0], arrived[0], wide[0], band)
    shares = lax.all_to_all(shares, SRC, split_axis=0, concat_axis=0, tiled=True)
    return jnp.sum(shares.astype(jnp.float32), axis=0)


def solution(mesh):
    mesh = Mesh(mesh.devices.reshape(8, 2, 2, 2, 4), ("z", "yh", "core", "yl", "x"))
    both = TGT + SRC
    in_specs = (
        P(None, TGT),
        P(TGT),
        P(None, None, both),
        P(None, both),
        P(None, None, both),
        P(None, both),
        P(None, both),
        P(None, None, both),
        P(None, both),
        P(None, None, both),
        P(None, TGT),
        P(),
    )
    return jax.shard_map(
        per_device, mesh=mesh, in_specs=in_specs, out_specs=P(TGT, None), check_vma=False
    )
```

```python
import functools
import math

import jax
import jax.numpy as jnp
import numpy as np
from jax import lax
from jax.experimental import pallas as pl
from jax.experimental.pallas import tpu as pltpu
from jax.sharding import Mesh, PartitionSpec as P

HALO = 8
WAVE = 8.0
SMOOTH = 0.0025
TURN = WAVE / (2.0 * math.pi)
TURN_SQ = TURN * TURN

TGT = ("z", "yh", "core")
SRC = ("yl", "x")


def minimax(func, importance, terms, odd):
    nodes = 0.25 + 0.25 * np.cos(np.linspace(0.0, np.pi, 2001))
    nodes = nodes[nodes > 1e-6]
    scale = nodes if odd else np.ones_like(nodes)
    matter = importance(nodes)
    basis = np.stack([nodes ** (2 * k) for k in range(terms)], 1)
    value = func(nodes) / scale
    weight = np.ones_like(nodes)
    for _ in range(60):
        rows = scale * weight * matter
        coef = np.linalg.lstsq(basis * rows[:, None], value * rows, rcond=None)[0]
        error = np.abs((basis @ coef - value) * scale * matter)
        weight = weight * np.sqrt(1e-12 + error / error.max())
        weight = weight / weight.mean()
    return tuple(float(np.float32(c)) for c in coef)


SIN_POLY = minimax(lambda f: math.sqrt(2.0) * np.sin(np.pi * f), np.ones_like, 3, True)
COS_POLY = minimax(lambda f: math.sqrt(2.0) * np.cos(np.pi * f), lambda f: np.sin(np.pi * f), 3, False)
COS_LEAD = COS_POLY[-1]
COS_MONIC = tuple(c / COS_LEAD for c in COS_POLY[:-1]) + (1.0,)


def horner(z, coef):
    value = z + coef[-2] if coef[-1] == 1.0 else coef[-1] * z + coef[-2]
    for c in coef[-3::-1]:
        value = value * z + c
    return value


def split3(value):
    high = value.astype(jnp.bfloat16).astype(jnp.float32)
    rest = value - high
    mid = rest.astype(jnp.bfloat16).astype(jnp.float32)
    return high, mid, rest - mid


def payload_kernel(factor_ref, points_ref, weight_ref, basis_ref, span_ref, patch_ref, cweight_ref, coef_ref, target_ref, tweight_ref, out_ref, side_ref):
    rounds, controls = cweight_ref.shape
    count = points_ref.shape[2]
    label = lax.broadcasted_iota(jnp.int32, (controls, count), 0)
    pieces = []
    for s in range(rounds):
        span = span_ref[s : s + 1, :]
        patch = patch_ref[s : s + 1, :]
        column = jnp.transpose(jnp.broadcast_to(cweight_ref[s : s + 1, :], (8, controls)))[:, 0:1]
        scaled = []
        for a in range(3):
            picked = jnp.where(label == span + a, column, 0.0)
            scaled.append(basis_ref[a, s : s + 1, :] * jnp.sum(picked, axis=0, keepdims=True))
        denom = scaled[0] + scaled[1] + scaled[2]
        fre = jnp.zeros((1, count), jnp.float32)
        fim = jnp.zeros((1, count), jnp.float32)
        for p in range(factor_ref.shape[2]):
            fre = jnp.where(patch == p, factor_ref[s, 0, p], fre)
            fim = jnp.where(patch == p, factor_ref[s, 1, p], fim)
        weight = weight_ref[s : s + 1, :] / denom
        terms = [value * (weight * fre) for value in scaled] + [value * (weight * fim) for value in scaled]
        high = [t.astype(jnp.bfloat16).astype(jnp.float32) for t in terms]
        low = [t - h for t, h in zip(terms, high)]
        rows = [points_ref[c, s : s + 1, :].astype(jnp.float32) for c in range(3)] + [span.astype(jnp.float32)] + high + low
        pieces.append(jnp.concatenate(rows, axis=0))
    extra = jnp.concatenate(pieces, axis=0).astype(jnp.bfloat16)
    for copy in range(out_ref.shape[0]):
        out_ref[copy, : rounds * controls, :] = coef_ref[...]
        out_ref[copy, rounds * controls :, :] = extra
    parts = [target_ref[...].astype(jnp.float32), *split3(tweight_ref[...])]
    zero = jnp.zeros((2, target_ref.shape[1]), jnp.float32)
    side_ref[...] = jnp.concatenate(parts + [zero], axis=0).astype(jnp.bfloat16)


def source_payload(copies, factor, points, weight, basis, span, patch, cweight, coef, target, tweight):
    rounds, fields, controls = coef.shape
    count = points.shape[2]
    rows = rounds * controls + 16 * rounds
    points = jnp.transpose(points, (1, 0, 2))
    basis = jnp.transpose(basis, (1, 0, 2))
    coef = jnp.transpose(coef, (0, 2, 1)).reshape(rounds * controls, fields)
    vmem = pl.BlockSpec(memory_space=pltpu.VMEM)
    return pl.pallas_call(
        payload_kernel,
        in_specs=[pl.BlockSpec(memory_space=pltpu.SMEM)] + [vmem] * 9,
        out_specs=[vmem, vmem],
        out_shape=[
            jax.ShapeDtypeStruct((copies, rows, count), jnp.bfloat16),
            jax.ShapeDtypeStruct((8, target.shape[1]), jnp.bfloat16),
        ],
        name="payload",
    )(factor, points, weight, basis, span, patch, cweight, coef, target, tweight.reshape(1, -1))


def source_rows(gathered_ref, q, s, rounds, controls):
    first = rounds * controls + 16 * s
    return gathered_ref[q, first : first + 16, :].astype(jnp.float32)


def source_features(gathered_ref, q, rounds, controls):
    pieces = []
    for s in range(rounds):
        pos = source_rows(gathered_ref, q, s, rounds, controls)[0:3]
        norm = pos[0:1] * pos[0:1] + pos[1:2] * pos[1:2] + pos[2:3] * pos[2:3]
        parts = [pos, pos, pos, jnp.ones_like(pos), *split3(norm * TURN_SQ), jnp.zeros_like(norm)]
        pieces.append(jnp.concatenate(parts, axis=0).astype(jnp.bfloat16))
    return pieces


def source_density(gathered_ref, q, rounds, controls):
    count = gathered_ref.shape[2]
    label = lax.broadcasted_iota(jnp.int32, (controls, count), 0).astype(jnp.float32)
    pieces = []
    for s in range(rounds):
        rows = source_rows(gathered_ref, q, s, rounds, controls)
        masks = [label == rows[3:4] + float(a) for a in range(3)]
        spread = []
        for part in range(4):
            value = jnp.zeros((controls, count), jnp.float32)
            for a in range(3):
                value = jnp.where(masks[a], rows[4 + 3 * part + a : 5 + 3 * part + a], value)
            spread.append(value)
        spread = jnp.concatenate(spread, axis=0).astype(jnp.bfloat16)
        plain = gathered_ref[q, s * controls : (s + 1) * controls, :]
        half = plain.shape[1] // 2
        turned = jnp.concatenate([-plain[:, half:], plain[:, :half]], axis=1)
        matrix = jnp.concatenate([plain, turned, plain, turned], axis=0)
        value = lax.dot_general(spread, matrix, (((0,), (0,)), ((), ())), preferred_element_type=jnp.float32)
        pieces.append(value.astype(jnp.bfloat16))
    return jnp.concatenate(pieces, axis=0)


def widened(low, middle, high, rows, lanes):
    count = middle.shape[1]
    place = lax.broadcasted_iota(jnp.int32, (8, lanes), 1)

    def moved(value, shift):
        pad = jnp.concatenate([value, jnp.zeros((8, lanes - count), jnp.float32)], axis=1)
        return pltpu.roll(pad, shift % lanes, 1)

    inner = jnp.where(place < HALO + count, moved(middle, HALO), moved(high, HALO + count))
    outer = jnp.where(place < HALO, moved(low, HALO - count), inner)
    return jnp.where(place < rows, outer, 0.0)


def target_features(pos, rows):
    norm = pos[0:1] * pos[0:1] + pos[1:2] * pos[1:2] + pos[2:3] * pos[2:3] + SMOOTH
    scaled = [*split3(pos[0:3] * (-2.0 * TURN_SQ))]
    ones = jnp.ones((3, pos.shape[1]), jnp.float32)
    side = jnp.concatenate(scaled + [*split3(norm * TURN_SQ), ones, jnp.zeros_like(norm)], axis=0)
    return jnp.transpose(side)[:rows].astype(jnp.bfloat16)


def kernel_terms(square):
    inverse = lax.rsqrt(square)
    turns = square * inverse
    part = turns - jnp.round(turns)
    z = part * part
    sine = part * horner(z, SIN_POLY)
    cosine = horner(z, COS_MONIC)
    scaled = sine * inverse
    kre = (inverse - sine * scaled).astype(jnp.bfloat16)
    kim = (scaled * cosine).astype(jnp.bfloat16)
    return jnp.concatenate([kre, kim], axis=0)


def terms_kernel(first, make, rounds, controls, *refs):
    refs = list(refs)
    if first:
        core_ref, block_ref, other_ref, source_ref, out_ref, wide_ref, side_ref, total_ref = refs
        ready_ref = None
    elif make:
        wide_ref, source_ref, start_ref, out_ref, ready_ref, side_ref, total_ref = refs
    else:
        wide_ref, source_ref, start_ref, out_ref, side_ref, total_ref = refs
        ready_ref = source_ref
    tiles, rows, columns = out_ref.shape
    count = source_ref.shape[-1]
    width = rounds * count
    depth = width + 16 * rounds
    chunks = source_ref.shape[0] if make else source_ref.shape[0] // depth
    step = pl.program_id(0)

    @pl.when(step == 0)
    def _():
        if first:
            lanes = wide_ref.shape[2]
            low_core = core_ref[0] == 0
            block, across = block_ref[:8].astype(jnp.float32), block_ref[8:].astype(jnp.float32)
            other, beyond = other_ref[:8].astype(jnp.float32), other_ref[8:].astype(jnp.float32)
            pick = lambda a, b: jnp.where(low_core, a, b)
            wide_ref[0] = widened(pick(across, other), block, pick(other, across), rows, lanes)
            wide_ref[1] = widened(pick(block, beyond), other, pick(beyond, block), rows, lanes)
        for t in range(tiles):
            side_ref[t] = target_features(wide_ref[t], rows)
        total_ref[...] = jnp.zeros_like(total_ref)

    features, densities = {}, {}

    def squared(q, t):
        if q not in features:
            places = [slice(q * depth + width + 16 * s, q * depth + width + 16 * (s + 1)) for s in range(rounds)]
            if make:
                pieces = source_features(source_ref, q, rounds, controls)
                if ready_ref is not None:
                    for place, piece in zip(places, pieces):
                        ready_ref[place, :] = piece
            else:
                pieces = [ready_ref[place, :] for place in places]
            features[q] = jnp.concatenate(pieces, axis=1)
        return jnp.dot(side_ref[t], features[q], preferred_element_type=jnp.float32)

    def density(q):
        if q not in densities:
            place = slice(q * depth, q * depth + width)
            if make:
                densities[q] = source_density(source_ref, q, rounds, controls)
                if ready_ref is not None:
                    ready_ref[place, :] = densities[q]
            else:
                densities[q] = ready_ref[place, :]
        return densities[q]

    def add(terms, q, t):
        total_ref[t] += jnp.dot(terms, density(q), preferred_element_type=jnp.float32)

    items = [(q, t) for q in range(chunks) for t in range(tiles)]
    square = squared(*items[0])
    waiting = None
    for n, (q, t) in enumerate(items):
        later = squared(*items[n + 1]) if n + 1 < len(items) else None
        density(q)
        terms = kernel_terms(square)
        if waiting is not None:
            add(*waiting)
        waiting, square = (terms, q, t), later
    add(*waiting)

    @pl.when(step == pl.num_programs(0) - 1)
    def _():
        for t in range(tiles):
            plain = total_ref[t, :rows]
            other = total_ref[t, rows:] * COS_LEAD
            half = columns // 2
            out = plain + jnp.concatenate([-other[:, half:], other[:, :half]], axis=1)
            if not first:
                out = out + start_ref[t]
            out_ref[t] = out


def kernel_sums(rows, lanes, sources, rounds, controls, make, blocks=None, wide=None, start=None, tile=0):
    first = blocks is not None
    tiles = 2 if first else 1
    count = sources.shape[-1]
    chunk = rounds * count + 16 * rounds
    per_step = 8 if make and not first else 4
    if make:
        chunks = sources.shape[0]
        source_spec = pl.BlockSpec((per_step,) + sources.shape[1:], lambda i: (i, 0, 0))
    else:
        chunks = sources.shape[0] // chunk
        source_spec = pl.BlockSpec((per_step * chunk, count), lambda i: (i, 0))
    out_specs = [pl.BlockSpec((tiles, rows, count), lambda i: (0, 0, 0))]
    out_shape = [jax.ShapeDtypeStruct((tiles, rows, count), jnp.float32)]
    if first:
        core, block, other = blocks
        whole = pl.BlockSpec(block.shape, lambda i: (0, 0))
        in_specs = [pl.BlockSpec(memory_space=pltpu.SMEM), whole, whole, source_spec]
        args = [core, block, other, sources]
        out_specs.append(pl.BlockSpec((2, 8, lanes), lambda i: (0, 0, 0)))
        out_shape.append(jax.ShapeDtypeStruct((2, 8, lanes), jnp.float32))
    else:
        in_specs = [
            pl.BlockSpec((1, 8, lanes), lambda i: (tile, 0, 0)),
            source_spec,
            pl.BlockSpec((1, rows, count), lambda i: (tile, 0, 0)),
        ]
        args = [wide, sources, start]
        if make:
            out_specs.append(pl.BlockSpec((per_step * chunk, count), lambda i: (i, 0)))
            out_shape.append(jax.ShapeDtypeStruct((chunks * chunk, count), jnp.bfloat16))
    pairs = tiles * rows * chunks * rounds * count
    return pl.pallas_call(
        functools.partial(terms_kernel, first, make, rounds, controls),
        grid=(chunks // per_step,),
        in_specs=in_specs,
        out_specs=out_specs,
        out_shape=out_shape,
        scratch_shapes=[
            pltpu.VMEM((tiles, rows, 16), jnp.bfloat16),
            pltpu.VMEM((tiles, 2 * rows, count), jnp.float32),
        ],
        compiler_params=pltpu.CompilerParams(vmem_limit_bytes=24 << 20),
        cost_estimate=pl.CostEstimate(flops=pairs * count * 8, bytes_accessed=1 << 20, transcendentals=pairs),
        name="terms",
    )(*args)


def band_kernel(scale, offsets_ref, own_ref, arrived_ref, side_ref, band_ref, out_ref, pot_ref):
    rows = own_ref.shape[0]
    columns = own_ref.shape[1]
    block = band_ref.shape[1]
    side = side_ref[...]
    weight = (side[3:4] + side[4:5]) + side[5:6]
    weight = jnp.transpose(jnp.broadcast_to(weight * scale, (8, weight.shape[1])))[:rows, 0:1]
    pot_ref[...] = (own_ref[...] + arrived_ref[...]) * weight
    factors = jnp.transpose(band_ref[...])
    shell = pot_ref[HALO : HALO + block, :]
    for diag in range(band_ref.shape[0]):
        shifted = pot_ref[pl.ds(HALO + offsets_ref[diag], block), :]
        shell = shell + factors[:, diag : diag + 1] * shifted
    shell = shell.astype(jnp.bfloat16)
    for copy in range(out_ref.shape[0]):
        out_ref[copy] = shell


def band_shares(copies, scale, offsets, own, arrived, side, band):
    vmem = pl.BlockSpec(memory_space=pltpu.VMEM)
    block, columns = band.shape[1], own.shape[1]
    return pl.pallas_call(
        functools.partial(band_kernel, scale),
        in_specs=[pl.BlockSpec(memory_space=pltpu.SMEM)] + [vmem] * 4,
        out_specs=vmem,
        out_shape=jax.ShapeDtypeStruct((copies, block, columns), jnp.bfloat16),
        scratch_shapes=[pltpu.VMEM(own.shape, jnp.float32)],
        compiler_params=pltpu.CompilerParams(vmem_limit_bytes=16 << 20),
        name="band",
    )(offsets, own, arrived, side, band)


def per_device(
    tgt_points, tgt_weight, src_points, src_weight, basis, span, patch, patch_factor, ctrl_weight, ctrl_coef, band, offsets
):
    rows = tgt_points.shape[1]
    rounds, columns, controls = ctrl_coef.shape
    zs = lax.axis_size("z")
    groups = lax.axis_size(SRC)
    blocks = lax.axis_size(TGT)
    swap = [(0, 1), (1, 0)]

    sent, side = source_payload(
        zs, patch_factor, src_points, src_weight, basis, span, patch, ctrl_weight, ctrl_coef, tgt_points, tgt_weight
    )
    links = [(k, k + 1) for k in range(1, blocks - 1, 2)]
    across = lax.ppermute(side, TGT, links + [(b, a) for a, b in links])
    gathered = lax.all_to_all(sent, "z", split_axis=0, concat_axis=0, tiled=True)
    block = jnp.concatenate([side, across], axis=0)
    other = lax.ppermute(block, "core", swap)
    core = lax.axis_index("core").astype(jnp.int32).reshape(1)

    span_rows = rows + 2 * HALO
    lanes = -(-span_rows // 128) * 128
    gathered2 = lax.ppermute(gathered, "yh", swap)
    shapes = (span_rows, lanes)
    sums, wide = kernel_sums(*shapes, gathered, rounds, controls, True, blocks=(core, block, other))
    share, made = kernel_sums(*shapes, gathered2, rounds, controls, True, wide=wide, start=sums, tile=1)
    arrived = lax.ppermute(share, "core", swap)
    (own,) = kernel_sums(*shapes, made, rounds, controls, False, wide=wide, start=sums, tile=0)

    source_count = rounds * src_weight.shape[1] * blocks * groups
    scale = TURN / math.sqrt(source_count)
    shares = band_shares(groups, scale, offsets, own[0], arrived[0], wide[0], band)
    shares = lax.all_to_all(shares, SRC, split_axis=0, concat_axis=0, tiled=True)
    return jnp.sum(shares.astype(jnp.float32), axis=0)


def solution(mesh):
    mesh = Mesh(mesh.devices.reshape(8, 2, 2, 2, 4), ("z", "yh", "core", "yl", "x"))
    both = TGT + SRC
    in_specs = (
        P(None, TGT),
        P(TGT),
        P(None, None, both),
        P(None, both),
        P(None, None, both),
        P(None, both),
        P(None, both),
        P(None, None, both),
        P(None, both),
        P(None, None, both),
        P(None, TGT),
        P(),
    )
    return jax.shard_map(
        per_device, mesh=mesh, in_specs=in_specs, out_specs=P(TGT, None), check_vma=False
    )
```

```python
import functools
import math

import jax
import jax.numpy as jnp
import numpy as np
from jax import lax
from jax.experimental import pallas as pl
from jax.experimental.pallas import tpu as pltpu
from jax.sharding import Mesh, PartitionSpec as P

HALO = 8
WAVE = 8.0
SMOOTH = 0.0025
TURN = WAVE / (2.0 * math.pi)
TURN_SQ = TURN * TURN

TGT = ("z", "yh", "core")
SRC = ("yl", "x")


def minimax(func, importance, terms, odd):
    nodes = 0.25 + 0.25 * np.cos(np.linspace(0.0, np.pi, 2001))
    nodes = nodes[nodes > 1e-6]
    scale = nodes if odd else np.ones_like(nodes)
    matter = importance(nodes)
    basis = np.stack([nodes ** (2 * k) for k in range(terms)], 1)
    value = func(nodes) / scale
    weight = np.ones_like(nodes)
    for _ in range(60):
        rows = scale * weight * matter
        coef = np.linalg.lstsq(basis * rows[:, None], value * rows, rcond=None)[0]
        error = np.abs((basis @ coef - value) * scale * matter)
        weight = weight * np.sqrt(1e-12 + error / error.max())
        weight = weight / weight.mean()
    return tuple(float(np.float32(c)) for c in coef)


SIN_POLY = minimax(lambda f: math.sqrt(2.0) * np.sin(np.pi * f), np.ones_like, 3, True)
COS_POLY = minimax(lambda f: math.sqrt(2.0) * np.cos(np.pi * f), lambda f: np.sin(np.pi * f), 3, False)
COS_LEAD = COS_POLY[-1]
COS_MONIC = tuple(c / COS_LEAD for c in COS_POLY[:-1]) + (1.0,)


def horner(z, coef):
    value = z + coef[-2] if coef[-1] == 1.0 else coef[-1] * z + coef[-2]
    for c in coef[-3::-1]:
        value = value * z + c
    return value


def split3(value):
    high = value.astype(jnp.bfloat16).astype(jnp.float32)
    rest = value - high
    mid = rest.astype(jnp.bfloat16).astype(jnp.float32)
    return high, mid, rest - mid


def payload_kernel(factor_ref, points_ref, weight_ref, basis_ref, span_ref, patch_ref, cweight_ref, coef_ref, target_ref, tweight_ref, out_ref, side_ref):
    rounds, controls = cweight_ref.shape
    count = points_ref.shape[2]
    label = lax.broadcasted_iota(jnp.int32, (controls, count), 0)
    pieces = []
    for s in range(rounds):
        span = span_ref[s : s + 1, :]
        patch = patch_ref[s : s + 1, :]
        column = jnp.transpose(jnp.broadcast_to(cweight_ref[s : s + 1, :], (8, controls)))[:, 0:1]
        scaled = []
        for a in range(3):
            picked = jnp.where(label == span + a, column, 0.0)
            scaled.append(basis_ref[a, s : s + 1, :] * jnp.sum(picked, axis=0, keepdims=True))
        denom = scaled[0] + scaled[1] + scaled[2]
        fre = jnp.zeros((1, count), jnp.float32)
        fim = jnp.zeros((1, count), jnp.float32)
        for p in range(factor_ref.shape[2]):
            fre = jnp.where(patch == p, factor_ref[s, 0, p], fre)
            fim = jnp.where(patch == p, factor_ref[s, 1, p], fim)
        weight = weight_ref[s : s + 1, :] / denom
        terms = [value * (weight * fre) for value in scaled] + [value * (weight * fim) for value in scaled]
        high = [t.astype(jnp.bfloat16).astype(jnp.float32) for t in terms]
        low = [t - h for t, h in zip(terms, high)]
        rows = [points_ref[c, s : s + 1, :].astype(jnp.float32) for c in range(3)] + [span.astype(jnp.float32)] + high + low
        pieces.append(jnp.concatenate(rows, axis=0))
    extra = jnp.concatenate(pieces, axis=0).astype(jnp.bfloat16)
    for copy in range(out_ref.shape[0]):
        out_ref[copy, : rounds * controls, :] = coef_ref[...]
        out_ref[copy, rounds * controls :, :] = extra
    parts = [target_ref[...].astype(jnp.float32), *split3(tweight_ref[...])]
    zero = jnp.zeros((2, target_ref.shape[1]), jnp.float32)
    side_ref[...] = jnp.concatenate(parts + [zero], axis=0).astype(jnp.bfloat16)


def source_payload(copies, factor, points, weight, basis, span, patch, cweight, coef, target, tweight):
    rounds, fields, controls = coef.shape
    count = points.shape[2]
    rows = rounds * controls + 16 * rounds
    points = jnp.transpose(points, (1, 0, 2))
    basis = jnp.transpose(basis, (1, 0, 2))
    coef = jnp.transpose(coef, (0, 2, 1)).reshape(rounds * controls, fields)
    vmem = pl.BlockSpec(memory_space=pltpu.VMEM)
    return pl.pallas_call(
        payload_kernel,
        in_specs=[pl.BlockSpec(memory_space=pltpu.SMEM)] + [vmem] * 9,
        out_specs=[vmem, vmem],
        out_shape=[
            jax.ShapeDtypeStruct((copies, rows, count), jnp.bfloat16),
            jax.ShapeDtypeStruct((8, target.shape[1]), jnp.bfloat16),
        ],
        name="payload",
    )(factor, points, weight, basis, span, patch, cweight, coef, target, tweight.reshape(1, -1))


def source_rows(gathered_ref, q, s, rounds, controls):
    first = rounds * controls + 16 * s
    return gathered_ref[q, first : first + 16, :].astype(jnp.float32)


def source_features(gathered_ref, q, rounds, controls):
    pieces = []
    for s in range(rounds):
        pos = source_rows(gathered_ref, q, s, rounds, controls)[0:3]
        norm = pos[0:1] * pos[0:1] + pos[1:2] * pos[1:2] + pos[2:3] * pos[2:3]
        parts = [pos, pos, pos, jnp.ones_like(pos), *split3(norm * TURN_SQ), jnp.zeros_like(norm)]
        pieces.append(jnp.concatenate(parts, axis=0).astype(jnp.bfloat16))
    return pieces


def source_density(gathered_ref, q, rounds, controls):
    count = gathered_ref.shape[2]
    label = lax.broadcasted_iota(jnp.int32, (controls, count), 0).astype(jnp.float32)
    pieces = []
    for s in range(rounds):
        rows = source_rows(gathered_ref, q, s, rounds, controls)
        masks = [label == rows[3:4] + float(a) for a in range(3)]
        spread = []
        for part in range(4):
            value = jnp.zeros((controls, count), jnp.float32)
            for a in range(3):
                value = jnp.where(masks[a], rows[4 + 3 * part + a : 5 + 3 * part + a], value)
            spread.append(value)
        spread = jnp.concatenate(spread, axis=0).astype(jnp.bfloat16)
        plain = gathered_ref[q, s * controls : (s + 1) * controls, :]
        half = plain.shape[1] // 2
        turned = jnp.concatenate([-plain[:, half:], plain[:, :half]], axis=1)
        matrix = jnp.concatenate([plain, turned, plain, turned], axis=0)
        value = lax.dot_general(spread, matrix, (((0,), (0,)), ((), ())), preferred_element_type=jnp.float32)
        pieces.append(value.astype(jnp.bfloat16))
    return jnp.concatenate(pieces, axis=0)


def widened(low, middle, high, rows, lanes):
    count = middle.shape[1]
    place = lax.broadcasted_iota(jnp.int32, (8, lanes), 1)

    def moved(value, shift):
        pad = jnp.concatenate([value, jnp.zeros((8, lanes - count), jnp.float32)], axis=1)
        return pltpu.roll(pad, shift % lanes, 1)

    inner = jnp.where(place < HALO + count, moved(middle, HALO), moved(high, HALO + count))
    outer = jnp.where(place < HALO, moved(low, HALO - count), inner)
    return jnp.where(place < rows, outer, 0.0)


def target_features(pos, rows):
    norm = pos[0:1] * pos[0:1] + pos[1:2] * pos[1:2] + pos[2:3] * pos[2:3] + SMOOTH
    scaled = [*split3(pos[0:3] * (-2.0 * TURN_SQ))]
    ones = jnp.ones((3, pos.shape[1]), jnp.float32)
    side = jnp.concatenate(scaled + [*split3(norm * TURN_SQ), ones, jnp.zeros_like(norm)], axis=0)
    return jnp.transpose(side)[:rows].astype(jnp.bfloat16)


def kernel_terms(square):
    inverse = lax.rsqrt(square)
    turns = square * inverse
    part = turns - jnp.round(turns)
    z = part * part
    sine = part * horner(z, SIN_POLY)
    cosine = horner(z, COS_MONIC)
    scaled = sine * inverse
    kre = (inverse - sine * scaled).astype(jnp.bfloat16)
    kim = (scaled * cosine).astype(jnp.bfloat16)
    return jnp.concatenate([kre, kim], axis=0)


def terms_kernel(first, make, rounds, controls, *refs):
    refs = list(refs)
    if first:
        core_ref, block_ref, other_ref, source_ref, out_ref, wide_ref, side_ref, total_ref = refs
        ready_ref = None
    elif make:
        wide_ref, source_ref, start_ref, out_ref, ready_ref, side_ref, total_ref = refs
    else:
        wide_ref, source_ref, start_ref, out_ref, side_ref, total_ref = refs
        ready_ref = source_ref
    tiles, rows, columns = out_ref.shape
    count = source_ref.shape[-1]
    width = rounds * count
    depth = width + 16 * rounds
    chunks = source_ref.shape[0] if make else source_ref.shape[0] // depth
    step = pl.program_id(0)

    @pl.when(step == 0)
    def _():
        if first:
            lanes = wide_ref.shape[2]
            low_core = core_ref[0] == 0
            block, across = block_ref[:8].astype(jnp.float32), block_ref[8:].astype(jnp.float32)
            other, beyond = other_ref[:8].astype(jnp.float32), other_ref[8:].astype(jnp.float32)
            pick = lambda a, b: jnp.where(low_core, a, b)
            wide_ref[0] = widened(pick(across, other), block, pick(other, across), rows, lanes)
            wide_ref[1] = widened(pick(block, beyond), other, pick(beyond, block), rows, lanes)
        for t in range(tiles):
            side_ref[t] = target_features(wide_ref[t], rows)
        total_ref[...] = jnp.zeros_like(total_ref)

    features, densities = {}, {}

    def squared(q, t):
        if q not in features:
            places = [slice(q * depth + width + 16 * s, q * depth + width + 16 * (s + 1)) for s in range(rounds)]
            if make:
                pieces = source_features(source_ref, q, rounds, controls)
                if ready_ref is not None:
                    for place, piece in zip(places, pieces):
                        ready_ref[place, :] = piece
            else:
                pieces = [ready_ref[place, :] for place in places]
            features[q] = jnp.concatenate(pieces, axis=1)
        return jnp.dot(side_ref[t], features[q], preferred_element_type=jnp.float32)

    def density(q):
        if q not in densities:
            place = slice(q * depth, q * depth + width)
            if make:
                densities[q] = source_density(source_ref, q, rounds, controls)
                if ready_ref is not None:
                    ready_ref[place, :] = densities[q]
            else:
                densities[q] = ready_ref[place, :]
        return densities[q]

    def add(terms, q, t):
        total_ref[t] += jnp.dot(terms, density(q), preferred_element_type=jnp.float32)

    items = [(q, t) for q in range(chunks) for t in range(tiles)]
    square = squared(*items[0])
    waiting = None
    for n, (q, t) in enumerate(items):
        later = squared(*items[n + 1]) if n + 1 < len(items) else None
        density(q)
        terms = kernel_terms(square)
        if waiting is not None:
            add(*waiting)
        waiting, square = (terms, q, t), later
    add(*waiting)

    @pl.when(step == pl.num_programs(0) - 1)
    def _():
        for t in range(tiles):
            plain = total_ref[t, :rows]
            other = total_ref[t, rows:] * COS_LEAD
            half = columns // 2
            out = plain + jnp.concatenate([-other[:, half:], other[:, :half]], axis=1)
            if not first:
                out = out + start_ref[t]
            out_ref[t] = out


def kernel_sums(rows, lanes, sources, rounds, controls, make, blocks=None, wide=None, start=None, tile=0):
    first = blocks is not None
    tiles = 2 if first else 1
    count = sources.shape[-1]
    chunk = rounds * count + 16 * rounds
    per_step = 8 if make and not first else 4
    if make:
        chunks = sources.shape[0]
        source_spec = pl.BlockSpec((per_step,) + sources.shape[1:], lambda i: (i, 0, 0))
    else:
        chunks = sources.shape[0] // chunk
        source_spec = pl.BlockSpec((per_step * chunk, count), lambda i: (i, 0))
    out_specs = [pl.BlockSpec((tiles, rows, count), lambda i: (0, 0, 0))]
    out_shape = [jax.ShapeDtypeStruct((tiles, rows, count), jnp.float32)]
    if first:
        core, block, other = blocks
        whole = pl.BlockSpec(block.shape, lambda i: (0, 0))
        in_specs = [pl.BlockSpec(memory_space=pltpu.SMEM), whole, whole, source_spec]
        args = [core, block, other, sources]
        out_specs.append(pl.BlockSpec((2, 8, lanes), lambda i: (0, 0, 0)))
        out_shape.append(jax.ShapeDtypeStruct((2, 8, lanes), jnp.float32))
    else:
        in_specs = [
            pl.BlockSpec((1, 8, lanes), lambda i: (tile, 0, 0)),
            source_spec,
            pl.BlockSpec((1, rows, count), lambda i: (tile, 0, 0)),
        ]
        args = [wide, sources, start]
        if make:
            out_specs.append(pl.BlockSpec((per_step * chunk, count), lambda i: (i, 0)))
            out_shape.append(jax.ShapeDtypeStruct((chunks * chunk, count), jnp.bfloat16))
    pairs = tiles * rows * chunks * rounds * count
    return pl.pallas_call(
        functools.partial(terms_kernel, first, make, rounds, controls),
        grid=(chunks // per_step,),
        in_specs=in_specs,
        out_specs=out_specs,
        out_shape=out_shape,
        scratch_shapes=[
            pltpu.VMEM((tiles, rows, 16), jnp.bfloat16),
            pltpu.VMEM((tiles, 2 * rows, count), jnp.float32),
        ],
        compiler_params=pltpu.CompilerParams(vmem_limit_bytes=24 << 20),
        cost_estimate=pl.CostEstimate(flops=pairs * count * 8, bytes_accessed=1 << 20, transcendentals=pairs),
        name="terms",
    )(*args)


def band_kernel(scale, offsets_ref, own_ref, arrived_ref, side_ref, band_ref, out_ref, pot_ref):
    rows = own_ref.shape[0]
    columns = own_ref.shape[1]
    block = band_ref.shape[1]
    side = side_ref[...]
    weight = (side[3:4] + side[4:5]) + side[5:6]
    weight = jnp.transpose(jnp.broadcast_to(weight * scale, (8, weight.shape[1])))[:rows, 0:1]
    pot_ref[...] = (own_ref[...] + arrived_ref[...]) * weight
    factors = jnp.transpose(band_ref[...])
    shell = pot_ref[HALO : HALO + block, :]
    for diag in range(band_ref.shape[0]):
        shifted = pot_ref[pl.ds(HALO + offsets_ref[diag], block), :]
        shell = shell + factors[:, diag : diag + 1] * shifted
    shell = shell.astype(jnp.bfloat16)
    for copy in range(out_ref.shape[0]):
        out_ref[copy] = shell


def band_shares(copies, scale, offsets, own, arrived, side, band):
    vmem = pl.BlockSpec(memory_space=pltpu.VMEM)
    block, columns = band.shape[1], own.shape[1]
    return pl.pallas_call(
        functools.partial(band_kernel, scale),
        in_specs=[pl.BlockSpec(memory_space=pltpu.SMEM)] + [vmem] * 4,
        out_specs=vmem,
        out_shape=jax.ShapeDtypeStruct((copies, block, columns), jnp.bfloat16),
        scratch_shapes=[pltpu.VMEM(own.shape, jnp.float32)],
        compiler_params=pltpu.CompilerParams(vmem_limit_bytes=16 << 20),
        name="band",
    )(offsets, own, arrived, side, band)


def per_device(
    tgt_points, tgt_weight, src_points, src_weight, basis, span, patch, patch_factor, ctrl_weight, ctrl_coef, band, offsets
):
    rows = tgt_points.shape[1]
    rounds, columns, controls = ctrl_coef.shape
    zs = lax.axis_size("z")
    groups = lax.axis_size(SRC)
    blocks = lax.axis_size(TGT)
    swap = [(0, 1), (1, 0)]

    sent, side = source_payload(
        zs, patch_factor, src_points, src_weight, basis, span, patch, ctrl_weight, ctrl_coef, tgt_points, tgt_weight
    )
    links = [(k, k + 1) for k in range(1, blocks - 1, 2)]
    across = lax.ppermute(side, TGT, links + [(b, a) for a, b in links])
    gathered = lax.all_to_all(sent, "z", split_axis=0, concat_axis=0, tiled=True)
    block = jnp.concatenate([side, across], axis=0)
    other = lax.ppermute(block, "core", swap)
    core = lax.axis_index("core").astype(jnp.int32).reshape(1)

    span_rows = rows + 2 * HALO
    lanes = -(-span_rows // 128) * 128
    gathered2 = lax.ppermute(gathered, "yh", swap)
    shapes = (span_rows, lanes)
    sums, wide = kernel_sums(*shapes, gathered, rounds, controls, True, blocks=(core, block, other))
    share, made = kernel_sums(*shapes, gathered2, rounds, controls, True, wide=wide, start=sums, tile=1)
    arrived = lax.ppermute(share, "core", swap)
    (own,) = kernel_sums(*shapes, made, rounds, controls, False, wide=wide, start=sums, tile=0)

    source_count = rounds * src_weight.shape[1] * blocks * groups
    scale = TURN / math.sqrt(source_count)
    shares = band_shares(groups, scale, offsets, own[0], arrived[0], wide[0], band)
    shares = lax.all_to_all(shares, SRC[::-1], split_axis=0, concat_axis=0, tiled=True)
    return jnp.sum(shares.astype(jnp.float32), axis=0)


def solution(mesh):
    mesh = Mesh(mesh.devices.reshape(8, 2, 2, 2, 4), ("z", "yh", "core", "yl", "x"))
    both = TGT + SRC
    in_specs = (
        P(None, TGT),
        P(TGT),
        P(None, None, both),
        P(None, both),
        P(None, None, both),
        P(None, both),
        P(None, both),
        P(None, None, both),
        P(None, both),
        P(None, None, both),
        P(None, TGT),
        P(),
    )
    return jax.shard_map(
        per_device, mesh=mesh, in_specs=in_specs, out_specs=P(TGT, None), check_vma=False
    )
```

```python
import functools
import math

import jax
import jax.numpy as jnp
import numpy as np
from jax import lax
from jax.experimental import pallas as pl
from jax.experimental.pallas import tpu as pltpu
from jax.sharding import Mesh, PartitionSpec as P

HALO = 8
WAVE = 8.0
SMOOTH = 0.0025
TURN = WAVE / (2.0 * math.pi)
TURN_SQ = TURN * TURN

LINE = ("zl", "zh")
TGT = ("zh", "zl", "yh", "core")
SRC = ("yl", "x")


def minimax(func, importance, terms, odd):
    nodes = 0.25 + 0.25 * np.cos(np.linspace(0.0, np.pi, 2001))
    nodes = nodes[nodes > 1e-6]
    scale = nodes if odd else np.ones_like(nodes)
    matter = importance(nodes)
    basis = np.stack([nodes ** (2 * k) for k in range(terms)], 1)
    value = func(nodes) / scale
    weight = np.ones_like(nodes)
    for _ in range(60):
        rows = scale * weight * matter
        coef = np.linalg.lstsq(basis * rows[:, None], value * rows, rcond=None)[0]
        error = np.abs((basis @ coef - value) * scale * matter)
        weight = weight * np.sqrt(1e-12 + error / error.max())
        weight = weight / weight.mean()
    return tuple(float(np.float32(c)) for c in coef)


SIN_POLY = minimax(lambda f: math.sqrt(2.0) * np.sin(np.pi * f), np.ones_like, 3, True)
COS_POLY = minimax(lambda f: math.sqrt(2.0) * np.cos(np.pi * f), lambda f: np.sin(np.pi * f), 3, False)
COS_LEAD = COS_POLY[-1]
COS_MONIC = tuple(c / COS_LEAD for c in COS_POLY[:-1]) + (1.0,)


def horner(z, coef):
    value = z + coef[-2] if coef[-1] == 1.0 else coef[-1] * z + coef[-2]
    for c in coef[-3::-1]:
        value = value * z + c
    return value


def split3(value):
    high = value.astype(jnp.bfloat16).astype(jnp.float32)
    rest = value - high
    mid = rest.astype(jnp.bfloat16).astype(jnp.float32)
    return high, mid, rest - mid


def payload_kernel(factor_ref, points_ref, weight_ref, basis_ref, span_ref, patch_ref, cweight_ref, coef_ref, target_ref, tweight_ref, out_ref, side_ref):
    rounds, controls = cweight_ref.shape
    count = points_ref.shape[2]
    label = lax.broadcasted_iota(jnp.int32, (controls, count), 0)
    pieces = []
    for s in range(rounds):
        span = span_ref[s : s + 1, :]
        patch = patch_ref[s : s + 1, :]
        column = jnp.transpose(jnp.broadcast_to(cweight_ref[s : s + 1, :], (8, controls)))[:, 0:1]
        scaled = []
        for a in range(3):
            picked = jnp.where(label == span + a, column, 0.0)
            scaled.append(basis_ref[a, s : s + 1, :] * jnp.sum(picked, axis=0, keepdims=True))
        denom = scaled[0] + scaled[1] + scaled[2]
        fre = jnp.zeros((1, count), jnp.float32)
        fim = jnp.zeros((1, count), jnp.float32)
        for p in range(factor_ref.shape[2]):
            fre = jnp.where(patch == p, factor_ref[s, 0, p], fre)
            fim = jnp.where(patch == p, factor_ref[s, 1, p], fim)
        weight = weight_ref[s : s + 1, :] / denom
        terms = [value * (weight * fre) for value in scaled] + [value * (weight * fim) for value in scaled]
        high = [t.astype(jnp.bfloat16).astype(jnp.float32) for t in terms]
        low = [t - h for t, h in zip(terms, high)]
        rows = [points_ref[c, s : s + 1, :].astype(jnp.float32) for c in range(3)] + [span.astype(jnp.float32)] + high + low
        pieces.append(jnp.concatenate(rows, axis=0))
    extra = jnp.concatenate(pieces, axis=0).astype(jnp.bfloat16)
    for copy in range(out_ref.shape[0]):
        out_ref[copy, : rounds * controls, :] = coef_ref[...]
        out_ref[copy, rounds * controls :, :] = extra
    parts = [target_ref[...].astype(jnp.float32), *split3(tweight_ref[...])]
    zero = jnp.zeros((2, target_ref.shape[1]), jnp.float32)
    side_ref[...] = jnp.concatenate(parts + [zero], axis=0).astype(jnp.bfloat16)


def source_payload(copies, factor, points, weight, basis, span, patch, cweight, coef, target, tweight):
    rounds, fields, controls = coef.shape
    count = points.shape[2]
    rows = rounds * controls + 16 * rounds
    points = jnp.transpose(points, (1, 0, 2))
    basis = jnp.transpose(basis, (1, 0, 2))
    coef = jnp.transpose(coef, (0, 2, 1)).reshape(rounds * controls, fields)
    vmem = pl.BlockSpec(memory_space=pltpu.VMEM)
    return pl.pallas_call(
        payload_kernel,
        in_specs=[pl.BlockSpec(memory_space=pltpu.SMEM)] + [vmem] * 9,
        out_specs=[vmem, vmem],
        out_shape=[
            jax.ShapeDtypeStruct((copies, rows, count), jnp.bfloat16),
            jax.ShapeDtypeStruct((8, target.shape[1]), jnp.bfloat16),
        ],
        name="payload",
    )(factor, points, weight, basis, span, patch, cweight, coef, target, tweight.reshape(1, -1))


def source_rows(gathered_ref, q, s, rounds, controls):
    first = rounds * controls + 16 * s
    return gathered_ref[q, first : first + 16, :].astype(jnp.float32)


def source_features(gathered_ref, q, rounds, controls):
    pieces = []
    for s in range(rounds):
        pos = source_rows(gathered_ref, q, s, rounds, controls)[0:3]
        norm = pos[0:1] * pos[0:1] + pos[1:2] * pos[1:2] + pos[2:3] * pos[2:3]
        parts = [pos, pos, pos, jnp.ones_like(pos), *split3(norm * TURN_SQ), jnp.zeros_like(norm)]
        pieces.append(jnp.concatenate(parts, axis=0).astype(jnp.bfloat16))
    return pieces


def source_density(gathered_ref, q, rounds, controls):
    count = gathered_ref.shape[2]
    label = lax.broadcasted_iota(jnp.int32, (controls, count), 0).astype(jnp.float32)
    pieces = []
    for s in range(rounds):
        rows = source_rows(gathered_ref, q, s, rounds, controls)
        masks = [label == rows[3:4] + float(a) for a in range(3)]
        spread = []
        for part in range(4):
            value = jnp.zeros((controls, count), jnp.float32)
            for a in range(3):
                value = jnp.where(masks[a], rows[4 + 3 * part + a : 5 + 3 * part + a], value)
            spread.append(value)
        spread = jnp.concatenate(spread, axis=0).astype(jnp.bfloat16)
        plain = gathered_ref[q, s * controls : (s + 1) * controls, :]
        half = plain.shape[1] // 2
        turned = jnp.concatenate([-plain[:, half:], plain[:, :half]], axis=1)
        matrix = jnp.concatenate([plain, turned, plain, turned], axis=0)
        value = lax.dot_general(spread, matrix, (((0,), (0,)), ((), ())), preferred_element_type=jnp.float32)
        pieces.append(value.astype(jnp.bfloat16))
    return jnp.concatenate(pieces, axis=0)


def widened(low, middle, high, rows, lanes):
    count = middle.shape[1]
    place = lax.broadcasted_iota(jnp.int32, (8, lanes), 1)

    def moved(value, shift):
        pad = jnp.concatenate([value, jnp.zeros((8, lanes - count), jnp.float32)], axis=1)
        return pltpu.roll(pad, shift % lanes, 1)

    inner = jnp.where(place < HALO + count, moved(middle, HALO), moved(high, HALO + count))
    outer = jnp.where(place < HALO, moved(low, HALO - count), inner)
    return jnp.where(place < rows, outer, 0.0)


def target_features(pos, rows):
    norm = pos[0:1] * pos[0:1] + pos[1:2] * pos[1:2] + pos[2:3] * pos[2:3] + SMOOTH
    scaled = [*split3(pos[0:3] * (-2.0 * TURN_SQ))]
    ones = jnp.ones((3, pos.shape[1]), jnp.float32)
    side = jnp.concatenate(scaled + [*split3(norm * TURN_SQ), ones, jnp.zeros_like(norm)], axis=0)
    return jnp.transpose(side)[:rows].astype(jnp.bfloat16)


def kernel_terms(square):
    inverse = lax.rsqrt(square)
    turns = square * inverse
    part = turns - jnp.round(turns)
    z = part * part
    sine = part * horner(z, SIN_POLY)
    cosine = horner(z, COS_MONIC)
    scaled = sine * inverse
    kre = (inverse - sine * scaled).astype(jnp.bfloat16)
    kim = (scaled * cosine).astype(jnp.bfloat16)
    return jnp.concatenate([kre, kim], axis=0)


def terms_kernel(first, make, rounds, controls, *refs):
    refs = list(refs)
    if first:
        core_ref, block_ref, other_ref, source_ref, out_ref, wide_ref, side_ref, total_ref = refs
        ready_ref = None
    elif make:
        wide_ref, source_ref, start_ref, out_ref, ready_ref, side_ref, total_ref = refs
    else:
        wide_ref, source_ref, start_ref, out_ref, side_ref, total_ref = refs
        ready_ref = source_ref
    tiles, rows, columns = out_ref.shape
    count = source_ref.shape[-1]
    width = rounds * count
    depth = width + 16 * rounds
    chunks = source_ref.shape[0] if make else source_ref.shape[0] // depth
    step = pl.program_id(0)

    @pl.when(step == 0)
    def _():
        if first:
            lanes = wide_ref.shape[2]
            low_core = core_ref[0] == 0
            block, across = block_ref[:8].astype(jnp.float32), block_ref[8:].astype(jnp.float32)
            other, beyond = other_ref[:8].astype(jnp.float32), other_ref[8:].astype(jnp.float32)
            pick = lambda a, b: jnp.where(low_core, a, b)
            wide_ref[0] = widened(pick(across, other), block, pick(other, across), rows, lanes)
            wide_ref[1] = widened(pick(block, beyond), other, pick(beyond, block), rows, lanes)
        for t in range(tiles):
            side_ref[t] = target_features(wide_ref[t], rows)
        total_ref[...] = jnp.zeros_like(total_ref)

    features, densities = {}, {}

    def squared(q, t):
        if q not in features:
            places = [slice(q * depth + width + 16 * s, q * depth + width + 16 * (s + 1)) for s in range(rounds)]
            if make:
                pieces = source_features(source_ref, q, rounds, controls)
                if ready_ref is not None:
                    for place, piece in zip(places, pieces):
                        ready_ref[place, :] = piece
            else:
                pieces = [ready_ref[place, :] for place in places]
            features[q] = jnp.concatenate(pieces, axis=1)
        return jnp.dot(side_ref[t], features[q], preferred_element_type=jnp.float32)

    def density(q):
        if q not in densities:
            place = slice(q * depth, q * depth + width)
            if make:
                densities[q] = source_density(source_ref, q, rounds, controls)
                if ready_ref is not None:
                    ready_ref[place, :] = densities[q]
            else:
                densities[q] = ready_ref[place, :]
        return densities[q]

    def add(terms, q, t):
        total_ref[t] += jnp.dot(terms, density(q), preferred_element_type=jnp.float32)

    items = [(q, t) for q in range(chunks) for t in range(tiles)]
    square = squared(*items[0])
    waiting = None
    for n, (q, t) in enumerate(items):
        later = squared(*items[n + 1]) if n + 1 < len(items) else None
        density(q)
        terms = kernel_terms(square)
        if waiting is not None:
            add(*waiting)
        waiting, square = (terms, q, t), later
    add(*waiting)

    @pl.when(step == pl.num_programs(0) - 1)
    def _():
        for t in range(tiles):
            plain = total_ref[t, :rows]
            other = total_ref[t, rows:] * COS_LEAD
            half = columns // 2
            out = plain + jnp.concatenate([-other[:, half:], other[:, :half]], axis=1)
            if not first:
                out = out + start_ref[t]
            out_ref[t] = out


def kernel_sums(rows, lanes, sources, rounds, controls, make, blocks=None, wide=None, start=None, tile=0):
    first = blocks is not None
    tiles = 2 if first else 1
    count = sources.shape[-1]
    chunk = rounds * count + 16 * rounds
    per_step = 8 if make and not first else 4
    if make:
        chunks = sources.shape[0]
        source_spec = pl.BlockSpec((per_step,) + sources.shape[1:], lambda i: (i, 0, 0))
    else:
        chunks = sources.shape[0] // chunk
        source_spec = pl.BlockSpec((per_step * chunk, count), lambda i: (i, 0))
    out_specs = [pl.BlockSpec((tiles, rows, count), lambda i: (0, 0, 0))]
    out_shape = [jax.ShapeDtypeStruct((tiles, rows, count), jnp.float32)]
    if first:
        core, block, other = blocks
        whole = pl.BlockSpec(block.shape, lambda i: (0, 0))
        in_specs = [pl.BlockSpec(memory_space=pltpu.SMEM), whole, whole, source_spec]
        args = [core, block, other, sources]
        out_specs.append(pl.BlockSpec((2, 8, lanes), lambda i: (0, 0, 0)))
        out_shape.append(jax.ShapeDtypeStruct((2, 8, lanes), jnp.float32))
    else:
        in_specs = [
            pl.BlockSpec((1, 8, lanes), lambda i: (tile, 0, 0)),
            source_spec,
            pl.BlockSpec((1, rows, count), lambda i: (tile, 0, 0)),
        ]
        args = [wide, sources, start]
        if make:
            out_specs.append(pl.BlockSpec((per_step * chunk, count), lambda i: (i, 0)))
            out_shape.append(jax.ShapeDtypeStruct((chunks * chunk, count), jnp.bfloat16))
    pairs = tiles * rows * chunks * rounds * count
    return pl.pallas_call(
        functools.partial(terms_kernel, first, make, rounds, controls),
        grid=(chunks // per_step,),
        in_specs=in_specs,
        out_specs=out_specs,
        out_shape=out_shape,
        scratch_shapes=[
            pltpu.VMEM((tiles, rows, 16), jnp.bfloat16),
            pltpu.VMEM((tiles, 2 * rows, count), jnp.float32),
        ],
        compiler_params=pltpu.CompilerParams(vmem_limit_bytes=24 << 20),
        cost_estimate=pl.CostEstimate(flops=pairs * count * 8, bytes_accessed=1 << 20, transcendentals=pairs),
        name="terms",
    )(*args)


def band_kernel(scale, offsets_ref, own_ref, arrived_ref, side_ref, band_ref, out_ref, pot_ref):
    rows = own_ref.shape[0]
    columns = own_ref.shape[1]
    block = band_ref.shape[1]
    side = side_ref[...]
    weight = (side[3:4] + side[4:5]) + side[5:6]
    weight = jnp.transpose(jnp.broadcast_to(weight * scale, (8, weight.shape[1])))[:rows, 0:1]
    pot_ref[...] = (own_ref[...] + arrived_ref[...]) * weight
    factors = jnp.transpose(band_ref[...])
    shell = pot_ref[HALO : HALO + block, :]
    for diag in range(band_ref.shape[0]):
        shifted = pot_ref[pl.ds(HALO + offsets_ref[diag], block), :]
        shell = shell + factors[:, diag : diag + 1] * shifted
    shell = shell.astype(jnp.bfloat16)
    for copy in range(out_ref.shape[0]):
        out_ref[copy] = shell


def band_shares(copies, scale, offsets, own, arrived, side, band):
    vmem = pl.BlockSpec(memory_space=pltpu.VMEM)
    block, columns = band.shape[1], own.shape[1]
    return pl.pallas_call(
        functools.partial(band_kernel, scale),
        in_specs=[pl.BlockSpec(memory_space=pltpu.SMEM)] + [vmem] * 4,
        out_specs=vmem,
        out_shape=jax.ShapeDtypeStruct((copies, block, columns), jnp.bfloat16),
        scratch_shapes=[pltpu.VMEM(own.shape, jnp.float32)],
        compiler_params=pltpu.CompilerParams(vmem_limit_bytes=16 << 20),
        name="band",
    )(offsets, own, arrived, side, band)


def per_device(
    tgt_points, tgt_weight, src_points, src_weight, basis, span, patch, patch_factor, ctrl_weight, ctrl_coef, band, offsets
):
    rows = tgt_points.shape[1]
    rounds, columns, controls = ctrl_coef.shape
    zs = lax.axis_size(LINE)
    groups = lax.axis_size(SRC)
    blocks = lax.axis_size(TGT)
    swap = [(0, 1), (1, 0)]

    sent, side = source_payload(
        zs, patch_factor, src_points, src_weight, basis, span, patch, ctrl_weight, ctrl_coef, tgt_points, tgt_weight
    )
    links = [(k, k + 1) for k in range(1, blocks - 1, 2)]
    across = lax.ppermute(side, TGT, links + [(b, a) for a, b in links])
    gathered = lax.all_to_all(sent, LINE, split_axis=0, concat_axis=0, tiled=True)
    block = jnp.concatenate([side, across], axis=0)
    other = lax.ppermute(block, "core", swap)
    core = lax.axis_index("core").astype(jnp.int32).reshape(1)

    span_rows = rows + 2 * HALO
    lanes = -(-span_rows // 128) * 128
    gathered2 = lax.ppermute(gathered, "yh", swap)
    shapes = (span_rows, lanes)
    sums, wide = kernel_sums(*shapes, gathered, rounds, controls, True, blocks=(core, block, other))
    share, made = kernel_sums(*shapes, gathered2, rounds, controls, True, wide=wide, start=sums, tile=1)
    arrived = lax.ppermute(share, "core", swap)
    (own,) = kernel_sums(*shapes, made, rounds, controls, False, wide=wide, start=sums, tile=0)

    source_count = rounds * src_weight.shape[1] * blocks * groups
    scale = TURN / math.sqrt(source_count)
    shares = band_shares(groups, scale, offsets, own[0], arrived[0], wide[0], band)
    shares = lax.all_to_all(shares, SRC[::-1], split_axis=0, concat_axis=0, tiled=True)
    return jnp.sum(shares.astype(jnp.float32), axis=0)


def solution(mesh):
    mesh = Mesh(mesh.devices.reshape(2, 4, 2, 2, 2, 4), ("zh", "zl", "yh", "core", "yl", "x"))
    both = TGT + SRC
    in_specs = (
        P(None, TGT),
        P(TGT),
        P(None, None, both),
        P(None, both),
        P(None, None, both),
        P(None, both),
        P(None, both),
        P(None, None, both),
        P(None, both),
        P(None, None, both),
        P(None, TGT),
        P(),
    )
    return jax.shard_map(
        per_device, mesh=mesh, in_specs=in_specs, out_specs=P(TGT, None), check_vma=False
    )
```
